512 devices in a mesh: dom: 32 (over y, x), plane: 16 (over z, core).
Axes of the slice: x: 4, y: 8, z: 8, core: 2. Of those that a mesh axis runs over, the one named last changes fastest.
Arguments:
- adjoint: float32 [3, 64, 9, 9, 1024], P(None, 'plane', None, None, 'dom'), may hold values from -6 to 6
- metric: float32 [4, 1024], P(None, 'dom'), may hold values from 0.5 to 2
- base_flow: float32 [2, 12, 5308416], P(None, None, ('dom', 'plane')), may hold values from -6 to 6
- edge_list: int32 [32, 5, 24], P('dom'), may hold values from -1 to 127, as said below
- flips: int32 [32, 5, 24], P('dom'), may hold values from 0 to 1, as said below
Outputs:
- adjoint_next: float32 [3, 64, 9, 9, 1024], P(None, 'plane', None, None, 'dom')
The draws below stay inside these ranges and needn't reach their ends.
Inputs may be any that keep to these rules, and one draw needn't show every extreme that they name: `edge_list`: entries are -1 or a local edge id j * 32 + l; no edge appears twice in one partition; filled slots come first in each block; a slot is filled exactly where its pair (as the steps define it) is filled, so block 2 has an even count; some block of some partition has all 24 slots filled, and every partition has an empty slot. `flips`: paired slots carry the same flag.
All inputs are finite; a program needn't handle non-finite values.
Results may differ from the reference program's by a relative error of at most 0.0003.
Values sent between devices are 32-bit elements; how exact they have to be, the bound alone decides.
A program may use at most 64 MiB of HBM per device.

```python
import jax
import jax.numpy as jnp
from jax import lax

NP = 9
MODES = 64
E_DEV = 32
CAP = 24
REACH = 2
STEPS = 2
PARTITIONS = 32
ELEMS = 1024
PTS_ALL = 82944
N_PLANE = 16


def pair_tables(key):
    blocks = 2 * REACH + 1
    raw_count = jax.random.randint(jax.random.fold_in(key, 1), (PARTITIONS, blocks), 1, CAP + 1)
    busy_rank = jax.random.randint(jax.random.fold_in(key, 3), (), 0, PARTITIONS)
    raw_count = raw_count.at[busy_rank, REACH + 1].set(CAP)
    self_count = 2 * jax.random.randint(jax.random.fold_in(key, 2), (PARTITIONS,), 0, CAP // 2)
    part_ids = jnp.arange(PARTITIONS, dtype=jnp.int32)[:, None]
    block_ids = jnp.arange(blocks, dtype=jnp.int32)[None, :]
    offset = block_ids - REACH
    canon_part = jnp.broadcast_to(jnp.where(offset > 0, part_ids, (part_ids + offset) % PARTITIONS), (PARTITIONS, blocks))
    canon_block = jnp.broadcast_to(jnp.where(offset > 0, block_ids, 2 * REACH - block_ids), (PARTITIONS, blocks))
    slot_count = raw_count[canon_part, canon_block]
    slot_count = jnp.where(offset == 0, self_count[:, None], slot_count)
    part_keys = jax.random.split(jax.random.fold_in(key, 4), PARTITIONS)
    orders = jax.vmap(lambda one_key: jax.random.permutation(one_key, 4 * E_DEV))(part_keys).astype(jnp.int32)
    chosen = jax.random.randint(jax.random.fold_in(key, 5), (PARTITIONS,), 0, blocks - 1)
    chosen = chosen + (chosen >= REACH).astype(jnp.int32)
    target = chosen * CAP
    found_at = jnp.argmax(orders == 4 * E_DEV - 1, axis=1)
    rows = jnp.arange(PARTITIONS, dtype=jnp.int32)
    moved = orders[rows, target]
    orders = orders.at[rows, found_at].set(moved)
    orders = orders.at[rows, target].set(4 * E_DEV - 1)
    edge_ids = orders[:, :blocks * CAP].reshape(PARTITIONS, blocks, CAP)
    slot_ids = jnp.arange(CAP, dtype=jnp.int32)[None, None, :]
    edge_table = jnp.where(slot_ids < slot_count[:, :, None], edge_ids, -1).astype(jnp.int32)
    raw_flip = jax.random.randint(jax.random.fold_in(key, 6), (PARTITIONS, blocks, CAP), 0, 2)
    canon_slot = jnp.broadcast_to(jnp.where(offset[:, :, None] == 0, slot_ids - slot_ids % 2, slot_ids), (PARTITIONS, blocks, CAP))
    flip_table = raw_flip[jnp.broadcast_to(canon_part[:, :, None], (PARTITIONS, blocks, CAP)), jnp.broadcast_to(canon_block[:, :, None], (PARTITIONS, blocks, CAP)), canon_slot]
    return (edge_table, flip_table.astype(jnp.int32))


def draw_edge_list(key, part):
    return pair_tables(key)[0]


def draw_flips(key, part):
    return pair_tables(key)[1]


def steps_of(stream_key, dims, cuts, low, high):
    loudness, own = 1.0, jax.random.fold_in(stream_key, 6)
    for axis_at, blocks in cuts:
        heights = jnp.exp(jax.random.uniform(jax.random.fold_in(own, axis_at), (blocks,), jnp.float32, low / len(cuts), high / len(cuts)))
        loudness = loudness * jnp.repeat(heights, dims[axis_at] // blocks).reshape([-1 if axis == axis_at else 1 for axis in range(len(dims))])
    return loudness


def centred(stream_key, dims, spread, reach, pieces=(), kind=jnp.bfloat16):
    entries = jax.random.normal(stream_key, dims, jnp.float32) * spread
    if len(pieces) > 0:
        entries = steps_of(stream_key, dims, pieces, -0.22, 0.18) * entries
    return jnp.clip(entries, min=-reach, max=reach).astype(kind)


def setup_inputs(seed: int = 0) -> dict:
    key_list = jax.random.split(jax.random.key(seed), 6)
    return {
        "adjoint": centred(key_list[0], (3, MODES, NP, NP, ELEMS), 1.0, 6.0, ((1, 16), (4, 32)), jnp.float32),
        "metric": jnp.clip(0.5 + 1.5 * jax.random.uniform(key_list[1], (4, ELEMS), jnp.float32) ** steps_of(key_list[1], (4, ELEMS), ((1, 32),), -0.2, 0.2), 0.5, 2.0),
        "base_flow": centred(key_list[2], (STEPS, 12, PTS_ALL * MODES), 1.0, 6.0, ((2, 512),), jnp.float32),
        "edge_list": draw_edge_list(jax.random.fold_in(key_list[5], 71), 0),
        "flips": draw_flips(jax.random.fold_in(key_list[5], 71), 0),
    }


step_size = 0.01
viscosity = 0.02


def cheb_table(node_count):
    order = node_count - 1
    node_ids = jnp.arange(node_count, dtype=jnp.int32)
    node_coords = -jnp.cos(jnp.pi * node_ids.astype(jnp.float32) / order)
    weight = jnp.where((node_ids == 0) | (node_ids == order), 2.0, 1.0).astype(jnp.float32)
    parity = jnp.where((node_ids[:, None] + node_ids[None, :]) % 2 == 0, 1.0, -1.0).astype(jnp.float32)
    on_diag = node_ids[:, None] == node_ids[None, :]
    differ = jnp.where(on_diag, 1.0, node_coords[:, None] - node_coords[None, :])
    off_diag = jnp.where(on_diag, 0.0, weight[:, None] / weight[None, :] * parity / differ)
    return off_diag - jnp.diag(jnp.sum(off_diag, axis=1))


def span_tables(modes):
    mode_ids = jnp.arange(modes, dtype=jnp.int32)
    wavenumber = (mode_ids + 1) // 2
    is_cosine = (mode_ids % 2 == 1) | (mode_ids == 0)
    span_ids = jnp.arange(modes, dtype=jnp.int32)
    phase_num = (span_ids[:, None] * wavenumber[None, :]) % modes
    angles = 2.0 * jnp.pi * phase_num.astype(jnp.float32) / modes
    cosines = jnp.cos(angles)
    sines = jnp.sin(angles)
    wave_f = wavenumber.astype(jnp.float32)
    span_basis = jnp.where(is_cosine[None, :], cosines, sines)
    span_slope = jnp.where(is_cosine[None, :], -wave_f[None, :] * sines, wave_f[None, :] * cosines)
    scaling = jnp.where((mode_ids == 0) | (mode_ids == modes - 1), 1.0 / modes, 2.0 / modes).astype(jnp.float32)
    forward = span_basis.T * scaling[:, None]
    return span_basis, span_slope, forward, wave_f * wave_f


def directional(field_data, metric, deriv_table, xi_row, eta_row):
    along_xi = jnp.einsum('ai,cmije->cmaje', deriv_table, field_data, precision=lax.Precision.HIGHEST)
    along_eta = jnp.einsum('bj,cmije->cmibe', deriv_table, field_data, precision=lax.Precision.HIGHEST)
    return metric[xi_row] * along_xi + metric[eta_row] * along_eta


def advect(coeffs, base_now, span_basis, span_slope, forward):
    values = jnp.einsum('nm,fmq->fnq', span_basis, coeffs, precision=lax.Precision.HIGHEST)
    along_z = jnp.einsum('nm,cmq->cnq', span_slope, coeffs[0:3], precision=lax.Precision.HIGHEST)
    products = []
    for comp in range(3):
        term = base_now[0] * values[3 + comp] + base_now[1] * values[6 + comp] + base_now[2] * along_z[comp]
        term = term - (values[0] * base_now[3 + comp] + values[1] * base_now[6 + comp] + values[2] * base_now[9 + comp])
        products.append(term)
    return jnp.einsum('mn,cnq->cmq', forward, jnp.stack(products), precision=lax.Precision.HIGHEST)


def accumulate(field_data, edge_sums, counts):
    node_count = field_data.shape[2]
    last = node_count - 1
    total = field_data
    total = total.at[:, :, :, 0, :].add(edge_sums[:, :, :, 0, :])
    total = total.at[:, :, last, :, :].add(edge_sums[:, :, :, 1, :])
    total = total.at[:, :, :, last, :].add(edge_sums[:, :, :, 2, :])
    total = total.at[:, :, 0, :, :].add(edge_sums[:, :, :, 3, :])
    weight = jnp.ones((node_count, node_count, field_data.shape[4]), jnp.float32)
    weight = weight.at[:, 0, :].add(counts[0][None, :])
    weight = weight.at[last, :, :].add(counts[1][None, :])
    weight = weight.at[:, last, :].add(counts[2][None, :])
    weight = weight.at[0, :, :].add(counts[3][None, :])
    return total / weight


def edge_traces(field_data):
    last = field_data.shape[2] - 1
    return jnp.stack([field_data[:, :, :, 0, :], field_data[:, :, last, :, :],
                      field_data[:, :, :, last, :], field_data[:, :, 0, :, :]], axis=3)


def assemble_all(field_data, edge_list, flips):
    components, modes, node_count, _, total_elems = field_data.shape
    partitions, blocks, capacity = edge_list.shape
    half_span = (blocks - 1) // 2
    elements = total_elems // partitions
    row_count = components * modes * node_count
    traces = edge_traces(field_data).reshape(components, modes, node_count, 4, partitions, elements)
    edge_table = jnp.transpose(traces, (4, 0, 1, 2, 3, 5)).reshape(partitions, row_count, 4 * elements)
    part_ids = jnp.arange(partitions, dtype=jnp.int32)[:, None, None]
    block_ids = jnp.arange(blocks, dtype=jnp.int32)[None, :, None]
    slot_ids = jnp.arange(capacity, dtype=jnp.int32)[None, None, :]
    shape3 = (partitions, blocks, capacity)
    partner = jnp.broadcast_to((part_ids + block_ids - half_span) % partitions, shape3)
    partner_block = jnp.broadcast_to(2 * half_span - block_ids, shape3)
    partner_slot = jnp.broadcast_to(jnp.where(block_ids == half_span, slot_ids + 1 - 2 * (slot_ids % 2), slot_ids), shape3)
    partner_edge = edge_list[partner, partner_block, partner_slot]
    gathered = edge_table[partner, :, jnp.maximum(partner_edge, 0)]
    gathered = gathered.reshape(partitions, blocks, capacity, components * modes, node_count)
    occupied = (edge_list >= 0).astype(jnp.float32)
    gathered = jnp.where((flips == 1)[..., None, None], gathered[..., ::-1], gathered) * occupied[..., None, None]
    gathered = gathered.reshape(partitions, blocks * capacity, row_count)
    slot_edges = edge_list.reshape(partitions, blocks * capacity)
    onehot = (slot_edges[:, :, None] == jnp.arange(4 * elements, dtype=jnp.int32)[None, None, :]).astype(jnp.float32)
    edge_sums = jnp.einsum('psr,pse->pre', gathered, onehot, precision=lax.Precision.HIGHEST)
    edge_sums = edge_sums.reshape(partitions, components, modes, node_count, 4, elements)
    edge_sums = jnp.transpose(edge_sums, (1, 2, 3, 4, 0, 5)).reshape(components, modes, node_count, 4, total_elems)
    counts = jnp.sum(onehot, axis=1).reshape(partitions, 4, elements)
    counts = jnp.transpose(counts, (1, 0, 2)).reshape(4, total_elems)
    return accumulate(field_data, edge_sums, counts)


def reference(adjoint, metric, base_flow, edge_list, flips):
    components, modes, node_count, _, total_elems = adjoint.shape
    partitions = edge_list.shape[0]
    elements = total_elems // partitions
    points = node_count * node_count * elements
    local_points = points // N_PLANE
    deriv_table = cheb_table(node_count)
    span_basis, span_slope, forward, wave_sq = span_tables(modes)
    adjoint_state = adjoint
    zero_index = jnp.zeros((), jnp.int32)
    for step_index in range(STEPS):
        grad_x = directional(adjoint_state, metric, deriv_table, 0, 2)
        grad_y = directional(adjoint_state, metric, deriv_table, 1, 3)
        stacked = jnp.concatenate([adjoint_state, grad_x, grad_y], axis=0)

        def physical(part_index, stacked=stacked, step_index=step_index):
            part_index = part_index.astype(jnp.int32)
            elem_start = (part_index * elements).astype(jnp.int32)
            coeffs = lax.dynamic_slice_in_dim(stacked, elem_start, elements, 4).reshape(9, modes, points)
            starts = (jnp.full((), step_index, jnp.int32), zero_index, (part_index * (modes * points)).astype(jnp.int32))
            base_flat = lax.dynamic_slice(base_flow, starts, (1, 12, modes * points))[0]
            base_now = jnp.transpose(base_flat.reshape(12, N_PLANE, modes, local_points), (0, 2, 1, 3)).reshape(12, modes, points)
            return advect(coeffs, base_now, span_basis, span_slope, forward).reshape(3, modes, node_count, node_count, elements)

        rates = lax.map(physical, jnp.arange(partitions, dtype=jnp.int32))
        returned = jnp.transpose(rates, (1, 2, 3, 4, 0, 5)).reshape(adjoint_state.shape)
        laplacian = directional(grad_x, metric, deriv_table, 0, 2) + directional(grad_y, metric, deriv_table, 1, 3)
        updated = adjoint_state + step_size * (returned + viscosity * (laplacian - wave_sq[None, :, None, None, None] * adjoint_state))
        adjoint_state = assemble_all(updated, edge_list, flips)
    return adjoint_state
```

```python
import functools

import jax
import jax.numpy as jnp
import ml_dtypes
import numpy as np
from jax import lax
from jax.experimental import pallas as pl
from jax.experimental.pallas import tpu as pltpu
from jax.sharding import PartitionSpec as P

MODES = 64
STEPS = 2
NODES = 9
NPTS = NODES * NODES
ELEMS = 32
PLANE = 16
LOCAL = MODES // PLANE
SPAN_PTS = NPTS * ELEMS // PLANE
CAP = 24
REACH = 2
STEP_SIZE = 0.01
VISCOSITY = 0.02

ROWS = 88
KROWS = 96
WIRE = 56
BACK = 24
LEAD = 8
BASE_ROWS = 12 * NPTS * STEPS

F32 = jnp.float32
BF16 = jnp.bfloat16
MESH_ID = pl.DeviceIdType.MESH


def split_table(table):
    hi = table.astype(np.float32).astype(ml_dtypes.bfloat16)
    lo = (table - hi.astype(np.float64)).astype(np.float32).astype(ml_dtypes.bfloat16)
    return np.concatenate([hi, hi, lo], axis=1)


def derivative_tables():
    order = NODES - 1
    ids = np.arange(NODES)
    coords = -np.cos(np.pi * ids / order)
    weight = np.where((ids == 0) | (ids == order), 2.0, 1.0)
    table = np.zeros((NODES, NODES))
    for a in range(NODES):
        for i in range(NODES):
            if a != i:
                table[a, i] = weight[a] / weight[i] * (-1.0) ** (a + i) / (coords[a] - coords[i])
    table -= np.diag(table.sum(axis=1))
    eye = np.eye(NODES)
    along_xi, along_eta = np.kron(table, eye), np.kron(eye, table)
    ops = [
        along_xi,
        along_eta,
        along_xi @ along_xi,
        along_xi @ along_eta,
        along_eta @ along_eta,
    ]
    stacked = np.zeros((len(ops) * ROWS, KROWS))
    for at, op in enumerate(ops):
        stacked[at * ROWS : at * ROWS + NPTS, :NPTS] = op
    return split_table(stacked)


def span_tables():
    modes = np.arange(MODES)
    wave = (modes + 1) // 2
    cosine = (modes % 2 == 1) | (modes == 0)
    angles = 2.0 * np.pi * ((np.arange(MODES)[:, None] * wave[None, :]) % MODES) / MODES
    basis = np.where(cosine[None, :], np.cos(angles), np.sin(angles))
    slope = np.where(cosine[None, :], -wave * np.sin(angles), wave * np.cos(angles))
    scale = np.where((modes == 0) | (modes == MODES - 1), 1.0 / MODES, 2.0 / MODES)
    forward = basis.T * scale[:, None]
    order = (np.arange(PLANE)[None, :] * LOCAL + np.arange(LOCAL)[:, None]).reshape(-1)
    span = np.concatenate([basis[:, order], slope[:, order]], axis=0)
    return split_table(span), split_table(forward[order])


def halves(x):
    hi = x.astype(BF16)
    return hi, (x - hi.astype(F32)).astype(BF16)


def three(x):
    hi, lo = halves(x)
    return jnp.concatenate([hi, lo, hi], axis=0)


def dot(a, b):
    return jnp.dot(a, b, preferred_element_type=F32)


def swap_blocks(parts):
    shape = parts[0].shape
    lane = lax.broadcasted_iota(jnp.int32, shape, 1)
    even = (lane // 32) % 2 == 0
    low = lane < 64
    a0, a1, a2, a3 = parts

    def near(x, y):
        return (
            jnp.where(even, x, pltpu.roll(y, 32, 1)),
            jnp.where(even, pltpu.roll(x, 96, 1), y),
        )

    def far(x, y):
        moved = pltpu.roll(jnp.where(low, y, x), 64, 1)
        return jnp.where(low, x, moved), jnp.where(low, moved, y)

    b0, b1 = near(a0, a1)
    b2, b3 = near(a2, a3)
    c0, c2 = far(b0, b2)
    c1, c3 = far(b1, b3)
    return [c0, c1, c2, c3]


def head(field):
    return [(field, k) for k in range(4)]


def tail(first, second):
    pair = [(first, 4), (first, 5)]
    return pair + ([(second, 4), (second, 5)] if second is not None else [None, None])


OUT_BLOCKS = (
    [head(0), head(1), head(2), tail(0, 1), tail(2, 3)]
    + [head(3), head(4), head(5), head(6), head(7), head(8)]
    + [tail(4, 5), tail(6, 7), tail(8, None)]
)
STATE_BLOCKS = 5
HEAD_AT = {0: 0, 1: 1, 2: 2, 3: 5, 4: 6, 5: 7, 6: 8, 7: 9, 8: 10}
TAIL_AT = {0: (3, 0), 1: (3, 1), 2: (4, 0), 3: (4, 1), 4: (11, 0), 5: (11, 1), 6: (12, 0), 7: (12, 1), 8: (13, 0)}


def kernel(
    n_dom,
    adj_ref,
    met_ref,
    base_ref,
    edge_ref,
    flip_ref,
    deriv_ref,
    span_ref,
    fwd_ref,
    out_ref,
    state,
    grads,
    base_in,
    base_head,
    base_tail,
    send_out,
    recv_out,
    send_back,
    recv_back,
    edge_out,
    edge_in,
    trace_a,
    trace_b,
    sums,
    send_hot,
    recv_hot,
    inv_weight,
    metrics,
    slot_ids,
    base_sem,
    out_send,
    out_recv,
    back_send,
    back_recv,
    edge_send,
    edge_recv,
):
    dom = lax.axis_index("dom")
    me = lax.axis_index("plane")

    barrier = pltpu.get_barrier_semaphore()

    def greet(distance, carry):
        pl.semaphore_signal(
            barrier, inc=1, device_id=(dom, lax.rem(me + distance, PLANE)), device_id_type=MESH_ID
        )
        return carry

    lax.fori_loop(1, PLANE, greet, 0)
    others = [block for block in range(2 * REACH + 1) if block != REACH]
    for block in others:
        pl.semaphore_signal(
            barrier,
            inc=1,
            device_id=(lax.rem(dom + block - REACH + n_dom, n_dom), me),
            device_id_type=MESH_ID,
        )

    base_copy = pltpu.make_async_copy(base_ref, base_in.at[pl.ds(LEAD, BASE_ROWS)], base_sem)
    base_copy.start()

    def out_copy(step, distance):
        peer = lax.rem(me + distance, PLANE)
        return pltpu.make_async_remote_copy(
            src_ref=send_out.at[step, pl.ds(pl.multiple_of(peer * WIRE, 8), WIRE)],
            dst_ref=recv_out.at[step, pl.ds(pl.multiple_of(me * WIRE, 8), WIRE)],
            send_sem=out_send.at[step, distance - 1],
            recv_sem=out_recv.at[step, distance - 1],
            device_id=(dom, peer),
            device_id_type=MESH_ID,
        )

    def back_copy(step, distance):
        peer = lax.rem(me + distance, PLANE)
        return pltpu.make_async_remote_copy(
            src_ref=send_back.at[step, pl.ds(pl.multiple_of(peer * BACK, 8), BACK)],
            dst_ref=recv_back.at[step, pl.ds(pl.multiple_of(me * BACK, 8), BACK)],
            send_sem=back_send.at[step, distance - 1],
            recv_sem=back_recv.at[step, distance - 1],
            device_id=(dom, peer),
            device_id_type=MESH_ID,
        )

    def edge_copy(step, block):
        return pltpu.make_async_remote_copy(
            src_ref=edge_out.at[step, pl.ds(block * CAP, CAP)],
            dst_ref=edge_in.at[step, pl.ds((2 * REACH - block) * CAP, CAP)],
            send_sem=edge_send.at[step, block],
            recv_sem=edge_recv.at[step, block],
            device_id=(lax.rem(dom + block - REACH + n_dom, n_dom), me),
            device_id_type=MESH_ID,
        )

    def each_peer(what):
        def body(distance, carry):
            what(distance)
            return carry

        lax.fori_loop(1, PLANE, body, 0)

    rows_ref = adj_ref
    for comp in range(3):
        for mode in range(LOCAL):
            state[comp, 0:NPTS, ELEMS * mode : ELEMS * (mode + 1)] = rows_ref[comp, :, mode, :]
        state[comp, NPTS:KROWS, :] = jnp.zeros((KROWS - NPTS, 128), F32)
    for row in range(4):
        for group in range(4):
            metrics[row : row + 1, ELEMS * group : ELEMS * (group + 1)] = met_ref[row : row + 1, :]
    xi_x, xi_y = metrics[0:1, :], metrics[1:2, :]
    eta_x, eta_y = metrics[2:3, :], metrics[3:4, :]

    lane_row = lax.broadcasted_iota(jnp.int32, (1, 128), 1)
    wave = ((LOCAL * me + lane_row // ELEMS + 1) // 2).astype(F32)

    def send_state(step):
        rhs = three(jnp.concatenate([state[0], state[1], state[2]], axis=1))
        first = dot(deriv_ref[0 : 2 * ROWS, :], rhs)
        for comp in range(3):
            lanes = slice(128 * comp, 128 * comp + 128)
            along_xi, along_eta = first[0:ROWS, lanes], first[ROWS : 2 * ROWS, lanes]
            grads[comp, 0:ROWS, :] = xi_x * along_xi + eta_x * along_eta
            grads[3 + comp, 0:ROWS, :] = xi_y * along_xi + eta_y * along_eta

        def nodes(which):
            if which is None:
                return jnp.zeros((PLANE, 128), F32)
            field, k = which
            rows = pl.ds(k, PLANE, stride=5)
            return state[field, rows, :] if field < 3 else grads[field - 3, rows, :]

        for at, block in enumerate(OUT_BLOCKS):
            for mode, rows in enumerate(swap_blocks([nodes(which) for which in block])):
                send_out[step, pl.ds(at * 4 + mode, PLANE, stride=WIRE), :] = rows
        if step == 0:
            pl.semaphore_wait(barrier, PLANE - 1 + len(others))
        each_peer(lambda distance: out_copy(step, distance).start())
        mine = pl.ds(pl.multiple_of(me * WIRE, 8), WIRE)
        recv_out[step, mine, :] = send_out[step, mine, :]

        second = dot(deriv_ref[2 * ROWS : 5 * ROWS, :], rhs)
        diffuse = STEP_SIZE * VISCOSITY
        keep = 1.0 - diffuse * (wave * wave)
        both_xi = diffuse * (xi_x * xi_x + xi_y * xi_y)
        mixed = (2.0 * diffuse) * (xi_x * eta_x + xi_y * eta_y)
        both_eta = diffuse * (eta_x * eta_x + eta_y * eta_y)
        for comp in range(3):
            lanes = slice(128 * comp, 128 * comp + 128)
            state[comp, 0:ROWS, :] = keep * state[comp, 0:ROWS, :] + (
                both_xi * second[0:ROWS, lanes]
                + mixed * second[ROWS : 2 * ROWS, lanes]
                + both_eta * second[2 * ROWS : 3 * ROWS, lanes]
            )

    def arrange_base():
        base_in[0:LEAD, :] = jnp.zeros((LEAD, 128), F32)
        base_in[LEAD + BASE_ROWS :, :] = jnp.zeros((LEAD, 128), F32)
        base_copy.wait()
        lane = lax.broadcasted_iota(jnp.int32, (12, 128), 1)
        in_head = lane >= 2 * me
        in_tail = lane < 2 * me + (SPAN_PTS - 128)

        def body(n, carry):
            start = SPAN_PTS * n - 2 * me + 128
            block = start // 128
            shift = start - 128 * block
            back = lax.rem(128 - shift, 128)
            early = lane < 128 - shift
            for step in range(STEPS):
                rolled = []
                for at in range(3):
                    row = LEAD + STEPS * (block - 1 + at) + step
                    rows = base_in[pl.ds(row, 12, stride=STEPS * NPTS), :]
                    rolled.append(pltpu.roll(rows, back, 1))
                to = pl.ds(n, 12, stride=MODES)
                base_head[step, to, :] = jnp.where(
                    in_head, jnp.where(early, rolled[0], rolled[1]), 0.0
                )
                base_tail[step, to, :] = jnp.where(
                    in_tail, jnp.where(early, rolled[1], rolled[2]), 0.0
                )
            return carry

        lax.fori_loop(0, MODES, body, 0)

    def prepare_edges():
        slot_ids[...] = jnp.full((16, 128), -1, jnp.int32)
        for block in range(2 * REACH + 1):
            lanes = slice(CAP * block, CAP * (block + 1))
            slot_ids[0:1, lanes] = edge_ref[block : block + 1, :]
            slot_ids[8:9, lanes] = flip_ref[block : block + 1, :]
        own, flip = slot_ids[0:1, :], slot_ids[8:9, :]
        odd = lane_row % 2 == 1
        paired = jnp.where(odd, pltpu.roll(own, 1, 1), pltpu.roll(own, 127, 1))
        inner = (lane_row >= CAP * REACH) & (lane_row < CAP * (REACH + 1))
        given = jnp.where(inner, paired, own)
        edge_row = lax.broadcasted_iota(jnp.int32, (128, 128), 0)
        hot = jnp.where(edge_row == own, 1.0, 0.0).astype(F32)
        recv_hot[:, 0:128] = hot.astype(BF16)
        recv_hot[:, 128:256] = hot.astype(BF16)
        gave = jnp.where(edge_row == given, 1.0, 0.0).astype(F32)
        turned = jnp.where(flip == 1, gave, 0.0)
        straight = (gave - turned).T.astype(BF16)
        turned = turned.T.astype(BF16)
        for part in range(2):
            send_hot[:, 256 * part : 256 * part + 128] = straight
            send_hot[:, 256 * part + 128 : 256 * part + 256] = turned
        counts = jnp.sum(hot.T, axis=0, keepdims=True)
        spread = []
        for edge in range(4):
            one = jnp.where(lane_row // ELEMS == edge, counts, 0.0)
            one = one + pltpu.roll(one, 64, 1)
            spread.append(one + pltpu.roll(one, 32, 1))
        inv_weight[...] = jnp.ones((KROWS, 128), F32)
        first_col, last_col = pl.ds(0, NODES, stride=NODES), pl.ds(8, NODES, stride=NODES)
        for rows, edge in ((first_col, 0), (slice(72, 81), 1), (last_col, 2), (slice(0, 9), 3)):
            inv_weight[rows, :] = inv_weight[rows, :] + spread[edge]
        inv_weight[...] = 1.0 / inv_weight[...]
        trace_b[...] = jnp.zeros((128, 256), F32)

    def physical(step):
        each_peer(lambda distance: out_copy(step, distance).wait_recv())
        columns = []
        for at in range(len(OUT_BLOCKS)):
            columns.append(
                jnp.concatenate(
                    [
                        recv_out[step, pl.ds(at * 4 + mode, PLANE, stride=WIRE), :]
                        for mode in range(LOCAL)
                    ],
                    axis=0,
                )
            )
        state_rhs = three(jnp.concatenate(columns[:STATE_BLOCKS], axis=1))
        grad_rhs = three(jnp.concatenate(columns[STATE_BLOCKS:], axis=1))
        of_state = dot(span_ref[...], state_rhs)
        of_grads = dot(span_ref[0:MODES, :], grad_rhs)

        def block_of(at, slope):
            if at < STATE_BLOCKS:
                rows = slice(MODES, 2 * MODES) if slope else slice(0, MODES)
                return of_state[rows, 128 * at : 128 * at + 128]
            at = at - STATE_BLOCKS
            return of_grads[:, 128 * at : 128 * at + 128]

        def head_of(field, slope=False):
            return block_of(HEAD_AT[field], slope)

        def tail_of(field, slope=False):
            at, side = TAIL_AT[field]
            both = block_of(at, slope)
            return pltpu.roll(both, 64, 1) if side else both

        def products(values, base):
            def flow(index):
                return base[step, MODES * index : MODES * (index + 1), :]

            state_now = [values(i) for i in range(3)]
            results = []
            for comp in range(3):
                term = (
                    flow(0) * values(3 + comp)
                    + flow(1) * values(6 + comp)
                    + flow(2) * values(comp, True)
                )
                results.append(
                    term
                    - (
                        state_now[0] * flow(3 + comp)
                        + state_now[1] * flow(6 + comp)
                        + state_now[2] * flow(9 + comp)
                    )
                )
            return results

        heads = products(head_of, base_head)
        tails = products(tail_of, base_tail)
        packed = heads + [tails[0] + pltpu.roll(tails[1], 64, 1), tails[2]]
        back = dot(fwd_ref[...], three(jnp.concatenate(packed, axis=1)))
        for at in range(5):
            for mode in range(LOCAL):
                send_back[step, pl.ds(at * 4 + mode, PLANE, stride=BACK), :] = back[
                    PLANE * mode : PLANE * (mode + 1), 128 * at : 128 * at + 128
                ]
        for mode in range(LOCAL):
            send_back[step, pl.ds(20 + mode, PLANE, stride=BACK), :] = jnp.zeros((PLANE, 128), F32)
        each_peer(lambda distance: back_copy(step, distance).start())
        mine = pl.ds(pl.multiple_of(me * BACK, 8), BACK)
        recv_back[step, mine, :] = send_back[step, mine, :]

    def update(step):
        each_peer(lambda distance: back_copy(step, distance).wait_recv())
        blocks = []
        for at in range(5):
            blocks.append(
                swap_blocks(
                    [
                        recv_back[step, pl.ds(at * 4 + mode, PLANE, stride=BACK), :]
                        for mode in range(LOCAL)
                    ]
                )
            )
        for comp in range(3):
            ends = blocks[3 + comp // 2][2 * (comp % 2) : 2 * (comp % 2) + 2]
            for k, rate in enumerate(blocks[comp] + ends):
                rows = pl.ds(k, PLANE, stride=5)
                state[comp, rows, :] = state[comp, rows, :] + STEP_SIZE * rate

    def exchange(step):
        first_col, last_col = pl.ds(0, NODES, stride=NODES), pl.ds(8, NODES, stride=NODES)
        edge_rows = (first_col, slice(72, 81), last_col, slice(0, 9))
        for comp in range(3):
            traces = swap_blocks([state[comp, rows, :] for rows in edge_rows])
            for mode in range(LOCAL):
                at = (comp * LOCAL + mode) * 16
                trace_a[at : at + NODES, :] = traces[mode]
        for i in range(NODES):
            rows = trace_a[pl.ds(i, 3 * LOCAL, stride=16), :]
            trace_b[12 * i : 12 * i + 12, 0:128] = rows
            trace_b[12 * (8 - i) : 12 * (8 - i) + 12, 128:256] = rows
        hi, lo = halves(trace_b[...])
        given = lax.dot_general(
            send_hot[...],
            jnp.concatenate([hi, lo], axis=1),
            (((1,), (1,)), ((), ())),
            preferred_element_type=F32,
        )
        edge_out[step] = given
        for block in others:
            edge_copy(step, block).start()
        inner = slice(CAP * REACH, CAP * (REACH + 1))
        edge_in[step, inner, :] = given[inner, :]
        edge_in[step, 120:128, :] = jnp.zeros((8, 128), F32)
        for block in others:
            edge_copy(step, block).wait_recv()
        hi, lo = halves(edge_in[step])
        sums[...] = dot(recv_hot[...], jnp.concatenate([hi, lo], axis=0)).T
        for comp in range(3):
            parts = swap_blocks(
                [sums[pl.ds(comp * LOCAL + mode, NODES, stride=12), :] for mode in range(LOCAL)]
            )
            for rows, part in zip(edge_rows, parts):
                state[comp, rows, :] = state[comp, rows, :] + part
            state[comp, 0:ROWS, :] = state[comp, 0:ROWS, :] * inv_weight[0:ROWS, :]

    for step in range(STEPS):
        send_state(step)
        if step == 0:
            prepare_edges()
            arrange_base()
        physical(step)
        update(step)
        exchange(step)

    for comp in range(3):
        for mode in range(LOCAL):
            out_ref[comp, :, mode, :] = state[comp, 0:NPTS, ELEMS * mode : ELEMS * (mode + 1)]

    for step in range(STEPS):
        each_peer(lambda distance, step=step: out_copy(step, distance).wait_send())
        each_peer(lambda distance, step=step: back_copy(step, distance).wait_send())
        for block in others:
            edge_copy(step, block).wait_send()


def shards(n_dom, adjoint, metric, base_flow, edge_list, flips):
    state_in = jnp.transpose(adjoint, (0, 2, 3, 1, 4)).reshape(3, NPTS, LOCAL, ELEMS)
    base_in = (
        base_flow.reshape(STEPS, 12, NPTS, 128).transpose(1, 2, 0, 3).reshape(BASE_ROWS, 128)
    )
    span, fwd = span_tables()
    vmem = pl.BlockSpec(memory_space=pltpu.VMEM)
    dma = pltpu.SemaphoreType.DMA
    result = pl.pallas_call(
        functools.partial(kernel, n_dom),
        out_shape=jax.ShapeDtypeStruct((3, NPTS, LOCAL, ELEMS), F32),
        in_specs=[vmem, vmem, pl.BlockSpec(memory_space=pl.ANY)] + [vmem] * 5,
        out_specs=vmem,
        scratch_shapes=[
            pltpu.VMEM((3, KROWS, 128), F32),
            pltpu.VMEM((6, KROWS, 128), F32),
            pltpu.VMEM((BASE_ROWS + 2 * LEAD, 128), F32),
            pltpu.VMEM((STEPS, 12 * MODES, 128), F32),
            pltpu.VMEM((STEPS, 12 * MODES, 128), F32),
            pltpu.VMEM((STEPS, PLANE * WIRE, 128), F32),
            pltpu.VMEM((STEPS, PLANE * WIRE, 128), F32),
            pltpu.VMEM((STEPS, PLANE * BACK, 128), F32),
            pltpu.VMEM((STEPS, PLANE * BACK, 128), F32),
            pltpu.VMEM((STEPS, 128, 128), F32),
            pltpu.VMEM((STEPS, 128, 128), F32),
            pltpu.VMEM((3 * LOCAL * 16, 128), F32),
            pltpu.VMEM((128, 256), F32),
            pltpu.VMEM((128, 128), F32),
            pltpu.VMEM((128, 512), BF16),
            pltpu.VMEM((128, 256), BF16),
            pltpu.VMEM((KROWS, 128), F32),
            pltpu.VMEM((8, 128), F32),
            pltpu.VMEM((16, 128), jnp.int32),
            dma(()),
            dma((STEPS, PLANE - 1)),
            dma((STEPS, PLANE - 1)),
            dma((STEPS, PLANE - 1)),
            dma((STEPS, PLANE - 1)),
            dma((STEPS, 2 * REACH + 1)),
            dma((STEPS, 2 * REACH + 1)),
        ],
        compiler_params=pltpu.CompilerParams(
            collective_id=0, has_side_effects=True, vmem_limit_bytes=40 * 1024 * 1024
        ),
    )(
        state_in,
        metric,
        base_in,
        edge_list[0],
        flips[0],
        jnp.asarray(derivative_tables()),
        jnp.asarray(span),
        jnp.asarray(fwd),
    )
    return jnp.transpose(result.reshape(3, NODES, NODES, LOCAL, ELEMS), (0, 3, 1, 2, 4))


def solution(mesh):
    placed = (
        P(None, "plane", None, None, "dom"),
        P(None, "dom"),
        P(None, None, ("dom", "plane")),
        P("dom", None, None),
        P("dom", None, None),
    )
    return jax.shard_map(
        functools.partial(shards, mesh.shape["dom"]),
        mesh=mesh,
        in_specs=placed,
        out_specs=P(None, "plane", None, None, "dom"),
        check_vma=False,
    )
```

```python
import functools

import jax
import jax.numpy as jnp
import ml_dtypes
import numpy as np
from jax import lax
from jax.experimental import pallas as pl
from jax.experimental.pallas import tpu as pltpu
from jax.sharding import PartitionSpec as P

MODES = 64
STEPS = 2
NODES = 9
NPTS = NODES * NODES
ELEMS = 32
PLANE = 16
LOCAL = MODES // PLANE
SPAN_PTS = NPTS * ELEMS // PLANE
CAP = 24
REACH = 2
STEP_SIZE = 0.01
VISCOSITY = 0.02

ROWS = 88
KROWS = 96
WIRE = 48
BACK = 16
REST = SPAN_PTS - 128
FLOWS = 12 * STEPS

F32 = jnp.float32
BF16 = jnp.bfloat16
MESH_ID = pl.DeviceIdType.MESH


def split_table(table):
    hi = table.astype(np.float32).astype(ml_dtypes.bfloat16)
    lo = (table - hi.astype(np.float64)).astype(np.float32).astype(ml_dtypes.bfloat16)
    return np.concatenate([hi, hi, lo], axis=1)


def derivative_tables():
    order = NODES - 1
    ids = np.arange(NODES)
    coords = -np.cos(np.pi * ids / order)
    weight = np.where((ids == 0) | (ids == order), 2.0, 1.0)
    table = np.zeros((NODES, NODES))
    for a in range(NODES):
        for i in range(NODES):
            if a != i:
                table[a, i] = weight[a] / weight[i] * (-1.0) ** (a + i) / (coords[a] - coords[i])
    table -= np.diag(table.sum(axis=1))
    eye = np.eye(NODES)
    along_xi, along_eta = np.kron(table, eye), np.kron(eye, table)
    ops = [
        along_xi,
        along_eta,
        along_xi @ along_xi,
        along_xi @ along_eta,
        along_eta @ along_eta,
    ]
    stacked = np.zeros((len(ops) * ROWS, KROWS))
    for at, op in enumerate(ops):
        stacked[at * ROWS : at * ROWS + NPTS, :NPTS] = op
    return split_table(stacked)


def span_tables():
    modes = np.arange(MODES)
    wave = (modes + 1) // 2
    cosine = (modes % 2 == 1) | (modes == 0)
    angles = 2.0 * np.pi * ((np.arange(MODES)[:, None] * wave[None, :]) % MODES) / MODES
    basis = np.where(cosine[None, :], np.cos(angles), np.sin(angles))
    slope = np.where(cosine[None, :], -wave * np.sin(angles), wave * np.cos(angles))
    scale = np.where((modes == 0) | (modes == MODES - 1), 1.0 / MODES, 2.0 / MODES)
    forward = basis.T * scale[:, None]
    order = (np.arange(PLANE)[None, :] * LOCAL + np.arange(LOCAL)[:, None]).reshape(-1)
    span = np.concatenate([basis[:, order], slope[:, order]], axis=0)
    return split_table(span), split_table(forward[order])


def halves(x):
    hi = x.astype(BF16)
    return hi, (x - hi.astype(F32)).astype(BF16)


def three(x):
    hi, lo = halves(x)
    return jnp.concatenate([hi, lo, hi], axis=0)


def dot(a, b):
    return jnp.dot(a, b, preferred_element_type=F32)


def swap_blocks(parts):
    shape = parts[0].shape
    lane = lax.broadcasted_iota(jnp.int32, shape, 1)
    even = (lane // 32) % 2 == 0
    low = lane < 64
    a0, a1, a2, a3 = parts

    def near(x, y):
        return (
            jnp.where(even, x, pltpu.roll(y, 32, 1)),
            jnp.where(even, pltpu.roll(x, 96, 1), y),
        )

    def far(x, y):
        moved = pltpu.roll(jnp.where(low, y, x), 64, 1)
        return jnp.where(low, x, moved), jnp.where(low, moved, y)

    b0, b1 = near(a0, a1)
    b2, b3 = near(a2, a3)
    c0, c2 = far(b0, b2)
    c1, c3 = far(b1, b3)
    return [c0, c1, c2, c3]


def turn(x, shift):
    return pltpu.roll(x, shift % 128, 1) if shift % 128 else x


STATE_BLOCKS = 4
HEAD_AT = (0, 1, 2, 4, 5, 6, 7, 8, 9)
TAIL_AT = (3, 10, 11)
DISTANCES = (8, 7, 9, 6, 10, 5, 11, 4, 12, 3, 13, 2, 14, 1, 15)


def kernel(
    n_dom,
    adj_ref,
    met_ref,
    base_ref,
    edge_ref,
    flip_ref,
    deriv_ref,
    span_ref,
    fwd_ref,
    out_ref,
    state,
    grads,
    base_in,
    base_rows,
    base_head,
    base_tail,
    send_out,
    recv_out,
    send_back,
    recv_back,
    edge_out,
    edge_in,
    trace_a,
    trace_b,
    sums,
    send_hot,
    recv_hot,
    inv_weight,
    metrics,
    slot_ids,
    adj_in,
    met_in,
    deriv_in,
    edge_ids,
    flip_ids,
    span_in,
    fwd_in,
    load_sem,
    out_send,
    out_recv,
    back_send,
    back_recv,
    edge_send,
    edge_recv,
):
    dom = lax.axis_index("dom")
    me = lax.axis_index("plane")

    barrier = pltpu.get_barrier_semaphore()

    def greet(distance, carry):
        pl.semaphore_signal(
            barrier, inc=1, device_id=(dom, lax.rem(me + distance, PLANE)), device_id_type=MESH_ID
        )
        return carry

    lax.fori_loop(1, PLANE, greet, 0)
    others = [block for block in range(2 * REACH + 1) if block != REACH]
    for block in others:
        pl.semaphore_signal(
            barrier,
            inc=1,
            device_id=(lax.rem(dom + block - REACH + n_dom, n_dom), me),
            device_id_type=MESH_ID,
        )

    loads = {}
    for at, (name, source, target) in enumerate(
        (
            ("state", adj_ref, adj_in),
            ("metric", met_ref, met_in),
            ("deriv", deriv_ref, deriv_in),
            ("base", base_ref, base_in),
            ("edges", edge_ref, edge_ids),
            ("flips", flip_ref, flip_ids),
            ("span", span_ref, span_in),
            ("forward", fwd_ref, fwd_in),
        )
    ):
        loads[name] = pltpu.make_async_copy(source, target, load_sem.at[at])
        loads[name].start()

    def out_copy(step, distance):
        peer = lax.rem(me + distance, PLANE)
        return pltpu.make_async_remote_copy(
            src_ref=send_out.at[step, pl.ds(pl.multiple_of(peer * WIRE, 8), WIRE)],
            dst_ref=recv_out.at[step, pl.ds(pl.multiple_of(me * WIRE, 8), WIRE)],
            send_sem=out_send.at[step, distance - 1],
            recv_sem=out_recv.at[step, distance - 1],
            device_id=(dom, peer),
            device_id_type=MESH_ID,
        )

    def back_copy(step, distance):
        peer = lax.rem(me + distance, PLANE)
        return pltpu.make_async_remote_copy(
            src_ref=send_back.at[step, pl.ds(pl.multiple_of(peer * BACK, 8), BACK)],
            dst_ref=recv_back.at[step, pl.ds(pl.multiple_of(me * BACK, 8), BACK)],
            send_sem=back_send.at[step, distance - 1],
            recv_sem=back_recv.at[step, distance - 1],
            device_id=(dom, peer),
            device_id_type=MESH_ID,
        )

    def edge_copy(step, block):
        return pltpu.make_async_remote_copy(
            src_ref=edge_out.at[step, pl.ds(block * CAP, CAP)],
            dst_ref=edge_in.at[step, pl.ds((2 * REACH - block) * CAP, CAP)],
            send_sem=edge_send.at[step, block],
            recv_sem=edge_recv.at[step, block],
            device_id=(lax.rem(dom + block - REACH + n_dom, n_dom), me),
            device_id_type=MESH_ID,
        )

    def each_peer(what):
        for distance in DISTANCES:
            what(distance)

    loads["state"].wait()
    for comp in range(3):
        for mode in range(LOCAL):
            state[comp, 0:NPTS, ELEMS * mode : ELEMS * (mode + 1)] = adj_in[comp, :, mode, :]
        state[comp, NPTS:KROWS, :] = jnp.zeros((KROWS - NPTS, 128), F32)
    loads["metric"].wait()
    for row in range(4):
        for group in range(4):
            metrics[row : row + 1, ELEMS * group : ELEMS * (group + 1)] = met_in[row : row + 1, :]
    xi_x, xi_y = metrics[0:1, :], metrics[1:2, :]
    eta_x, eta_y = metrics[2:3, :], metrics[3:4, :]

    lane_row = lax.broadcasted_iota(jnp.int32, (1, 128), 1)
    owner_lane = lax.broadcasted_iota(jnp.int32, (PLANE, 128), 1)
    owner_start = 2 * lax.broadcasted_iota(jnp.int32, (PLANE, 128), 0)
    after = owner_lane >= owner_start
    places = []
    for comp in range(3):
        place = (owner_lane - owner_start + (128 - REST * comp)) % 128
        places.append(place < REST)
    wave = ((LOCAL * me + lane_row // ELEMS + 1) // 2).astype(F32)

    def send_state(step):
        rhs = three(jnp.concatenate([state[0], state[1], state[2]], axis=1))
        if step == 0:
            loads["deriv"].wait()
        first = dot(deriv_in[0 : 2 * ROWS, :], rhs)
        for comp in range(3):
            lanes = slice(128 * comp, 128 * comp + 128)
            along_xi, along_eta = first[0:ROWS, lanes], first[ROWS : 2 * ROWS, lanes]
            grads[comp, 0:ROWS, :] = xi_x * along_xi + eta_x * along_eta
            grads[3 + comp, 0:ROWS, :] = xi_y * along_xi + eta_y * along_eta

        def nodes(field, k):
            rows = pl.ds(k, PLANE, stride=5)
            return state[field, rows, :] if field < 3 else grads[field - 3, rows, :]

        zeros = jnp.zeros((PLANE, 128), F32)

        def ends(first, second):
            parts = [nodes(first, 4), nodes(first, 5)]
            parts += [zeros, zeros] if second is None else [nodes(second, 4), nodes(second, 5)]
            return swap_blocks(parts)

        def put(at, mode, rows):
            send_out[step, pl.ds(at * 4 + mode, PLANE, stride=WIRE), :] = rows

        for group in range(3):
            fields = [3 * group + comp for comp in range(3)]
            early, late = ends(fields[0], fields[1]), ends(fields[2], None)
            packed = [zeros] * LOCAL
            for comp, field in enumerate(fields):
                heads = swap_blocks([nodes(field, k) for k in range(4)])
                both, side = (late, 0) if comp == 2 else (early, 64 * comp)
                for mode in range(LOCAL):
                    late_points = turn(both[mode], -side)
                    put(HEAD_AT[field], mode, jnp.where(after, heads[mode], late_points))
                    packed[mode] = jnp.where(
                        places[comp], turn(both[mode], REST * comp - side), packed[mode]
                    )
            for mode in range(LOCAL):
                put(TAIL_AT[group], mode, packed[mode])
        if step == 0:
            pl.semaphore_wait(barrier, PLANE - 1 + len(others))
        each_peer(lambda distance: out_copy(step, distance).start())
        mine = pl.ds(pl.multiple_of(me * WIRE, 8), WIRE)
        recv_out[step, mine, :] = send_out[step, mine, :]

        second = dot(deriv_in[2 * ROWS : 5 * ROWS, :], rhs)
        diffuse = STEP_SIZE * VISCOSITY
        keep = 1.0 - diffuse * (wave * wave)
        both_xi = diffuse * (xi_x * xi_x + xi_y * xi_y)
        mixed = (2.0 * diffuse) * (xi_x * eta_x + xi_y * eta_y)
        both_eta = diffuse * (eta_x * eta_x + eta_y * eta_y)
        for comp in range(3):
            lanes = slice(128 * comp, 128 * comp + 128)
            state[comp, 0:ROWS, :] = keep * state[comp, 0:ROWS, :] + (
                both_xi * second[0:ROWS, lanes]
                + mixed * second[ROWS : 2 * ROWS, lanes]
                + both_eta * second[2 * ROWS : 3 * ROWS, lanes]
            )

    def arrange_base():
        loads["base"].wait()

        def gather(block, carry):
            lanes = pl.ds(pl.multiple_of(128 * block, 128), 128)
            rows = pl.ds(pl.multiple_of(FLOWS * block, 8), FLOWS)
            base_rows[rows, :] = base_in[:, :, lanes].reshape(FLOWS, 128)
            return carry

        lax.fori_loop(0, NPTS, gather, 0)
        base_rows[FLOWS * NPTS :, :] = jnp.zeros((2 * FLOWS, 128), F32)
        lane = lax.broadcasted_iota(jnp.int32, (FLOWS, 128), 1)
        point = (lane - 2 * me + 128) % 128

        def body(n, carry):
            start = SPAN_PTS * n
            block = start // 128
            shift = start - 128 * block
            back = lax.rem(128 - shift + 2 * me, 128)
            early = point < 128 - shift
            rolled = []
            for at in range(3):
                rows = pl.ds(pl.multiple_of(FLOWS * (block + at), 8), FLOWS)
                rolled.append(pltpu.roll(base_rows[rows, :], back, 1))
            to = pl.ds(n, FLOWS, stride=MODES)
            base_head[to, :] = jnp.where(early, rolled[0], rolled[1])
            base_tail[to, :] = jnp.where(
                point < REST, jnp.where(early, rolled[1], rolled[2]), 0.0
            )
            return carry

        lax.fori_loop(0, MODES, body, 0)

    def prepare_edges():
        loads["edges"].wait()
        loads["flips"].wait()
        slot_ids[...] = jnp.full((16, 128), -1, jnp.int32)
        for block in range(2 * REACH + 1):
            lanes = slice(CAP * block, CAP * (block + 1))
            slot_ids[0:1, lanes] = edge_ids[block]
            slot_ids[8:9, lanes] = flip_ids[block]
        own, flip = slot_ids[0:1, :], slot_ids[8:9, :]
        odd = lane_row % 2 == 1
        paired = jnp.where(odd, pltpu.roll(own, 1, 1), pltpu.roll(own, 127, 1))
        inner = (lane_row >= CAP * REACH) & (lane_row < CAP * (REACH + 1))
        given = jnp.where(inner, paired, own)
        edge_row = lax.broadcasted_iota(jnp.int32, (128, 128), 0)
        hot = jnp.where(edge_row == own, 1.0, 0.0).astype(F32)
        recv_hot[:, 0:128] = hot.astype(BF16)
        recv_hot[:, 128:256] = hot.astype(BF16)
        gave = jnp.where(edge_row == given, 1.0, 0.0).astype(F32)
        turned = jnp.where(flip == 1, gave, 0.0)
        straight = (gave - turned).T.astype(BF16)
        turned = turned.T.astype(BF16)
        for part in range(2):
            send_hot[:, 256 * part : 256 * part + 128] = straight
            send_hot[:, 256 * part + 128 : 256 * part + 256] = turned
        counts = jnp.sum(hot.T, axis=0, keepdims=True)
        spread = []
        for edge in range(4):
            one = jnp.where(lane_row // ELEMS == edge, counts, 0.0)
            one = one + pltpu.roll(one, 64, 1)
            spread.append(one + pltpu.roll(one, 32, 1))
        inv_weight[...] = jnp.ones((KROWS, 128), F32)
        first_col, last_col = pl.ds(0, NODES, stride=NODES), pl.ds(8, NODES, stride=NODES)
        for rows, edge in ((first_col, 0), (slice(72, 81), 1), (last_col, 2), (slice(0, 9), 3)):
            inv_weight[rows, :] = inv_weight[rows, :] + spread[edge]
        inv_weight[...] = 1.0 / inv_weight[...]
        trace_b[...] = jnp.zeros((128, 256), F32)

    def physical(step):
        each_peer(lambda distance: out_copy(step, distance).wait_recv())
        columns = []
        for at in range(WIRE // LOCAL):
            columns.append(
                jnp.concatenate(
                    [
                        recv_out[step, pl.ds(at * 4 + mode, PLANE, stride=WIRE), :]
                        for mode in range(LOCAL)
                    ],
                    axis=0,
                )
            )
        state_rhs = three(jnp.concatenate(columns[:STATE_BLOCKS], axis=1))
        grad_rhs = three(jnp.concatenate(columns[STATE_BLOCKS:], axis=1))
        if step == 0:
            loads["span"].wait()
            loads["forward"].wait()
        of_state = dot(span_in[...], state_rhs)
        of_grads = dot(span_in[0:MODES, :], grad_rhs)

        def block_of(at, slope):
            if at < STATE_BLOCKS:
                rows = slice(MODES, 2 * MODES) if slope else slice(0, MODES)
                return of_state[rows, 128 * at : 128 * at + 128]
            at = at - STATE_BLOCKS
            return of_grads[:, 128 * at : 128 * at + 128]

        def head_of(field, slope=False):
            return block_of(HEAD_AT[field], slope)

        def tail_of(field, slope=False):
            packed = block_of(TAIL_AT[field // 3], slope)
            place = REST * (field % 3)
            return pltpu.roll(packed, 128 - place, 1) if place else packed

        def products(values, base):
            def flow(index):
                row = MODES * (STEPS * index + step)
                return base[row : row + MODES, :]

            state_now = [values(i) for i in range(3)]
            results = []
            for comp in range(3):
                term = (
                    flow(0) * values(3 + comp)
                    + flow(1) * values(6 + comp)
                    + flow(2) * values(comp, True)
                )
                results.append(
                    term
                    - (
                        state_now[0] * flow(3 + comp)
                        + state_now[1] * flow(6 + comp)
                        + state_now[2] * flow(9 + comp)
                    )
                )
            return results

        heads = products(head_of, base_head)
        tails = products(tail_of, base_tail)
        rest = tails[0] + pltpu.roll(tails[1], REST, 1) + pltpu.roll(tails[2], 2 * REST, 1)
        packed = heads + [rest]
        back = dot(fwd_in[...], three(jnp.concatenate(packed, axis=1)))
        for at in range(4):
            for mode in range(LOCAL):
                send_back[step, pl.ds(at * 4 + mode, PLANE, stride=BACK), :] = back[
                    PLANE * mode : PLANE * (mode + 1), 128 * at : 128 * at + 128
                ]
        each_peer(lambda distance: back_copy(step, distance).start())
        mine = pl.ds(pl.multiple_of(me * BACK, 8), BACK)
        recv_back[step, mine, :] = send_back[step, mine, :]

    def update(step):
        each_peer(lambda distance: back_copy(step, distance).wait_recv())
        def came(at, mode):
            return recv_back[step, pl.ds(at * 4 + mode, PLANE, stride=BACK), :]

        rest = [came(3, mode) for mode in range(LOCAL)]
        heads, ends = [], []
        for comp in range(3):
            firsts, lasts = [], []
            for mode in range(LOCAL):
                moved = came(comp, mode)
                last = jnp.where(places[0], turn(rest[mode], -REST * comp), 0.0)
                firsts.append(jnp.where(after, moved, 0.0))
                lasts.append(jnp.where(after, last, moved))
            heads.append(swap_blocks(firsts))
            ends.append(lasts)
        joined = [jnp.where(owner_lane < 64, x, pltpu.roll(y, 64, 1)) for x, y in zip(*ends[:2])]
        early, late = swap_blocks(joined), swap_blocks(ends[2])
        ends = (early[:2], early[2:], late[:2])
        for comp in range(3):
            for k, rate in enumerate(heads[comp] + ends[comp]):
                rows = pl.ds(k, PLANE, stride=5)
                state[comp, rows, :] = state[comp, rows, :] + STEP_SIZE * rate

    def exchange(step):
        first_col, last_col = pl.ds(0, NODES, stride=NODES), pl.ds(8, NODES, stride=NODES)
        edge_rows = (first_col, slice(72, 81), last_col, slice(0, 9))
        for comp in range(3):
            traces = swap_blocks([state[comp, rows, :] for rows in edge_rows])
            for mode in range(LOCAL):
                at = (comp * LOCAL + mode) * 16
                trace_a[at : at + NODES, :] = traces[mode]
        for i in range(NODES):
            rows = trace_a[pl.ds(i, 3 * LOCAL, stride=16), :]
            trace_b[12 * i : 12 * i + 12, 0:128] = rows
            trace_b[12 * (8 - i) : 12 * (8 - i) + 12, 128:256] = rows
        hi, lo = halves(trace_b[...])
        given = lax.dot_general(
            send_hot[...],
            jnp.concatenate([hi, lo], axis=1),
            (((1,), (1,)), ((), ())),
            preferred_element_type=F32,
        )
        edge_out[step] = given
        for block in others:
            edge_copy(step, block).start()
        inner = slice(CAP * REACH, CAP * (REACH + 1))
        edge_in[step, inner, :] = given[inner, :]
        edge_in[step, 120:128, :] = jnp.zeros((8, 128), F32)
        for block in others:
            edge_copy(step, block).wait_recv()
        hi, lo = halves(edge_in[step])
        sums[...] = dot(recv_hot[...], jnp.concatenate([hi, lo], axis=0)).T
        for comp in range(3):
            parts = swap_blocks(
                [sums[pl.ds(comp * LOCAL + mode, NODES, stride=12), :] for mode in range(LOCAL)]
            )
            for rows, part in zip(edge_rows, parts):
                state[comp, rows, :] = state[comp, rows, :] + part
            state[comp, 0:ROWS, :] = state[comp, 0:ROWS, :] * inv_weight[0:ROWS, :]

    for step in range(STEPS):
        send_state(step)
        if step == 0:
            prepare_edges()
            arrange_base()
        physical(step)
        update(step)
        exchange(step)

    for comp in range(3):
        for mode in range(LOCAL):
            out_ref[comp, :, mode, :] = state[comp, 0:NPTS, ELEMS * mode : ELEMS * (mode + 1)]

    for step in range(STEPS):
        each_peer(lambda distance, step=step: out_copy(step, distance).wait_send())
        each_peer(lambda distance, step=step: back_copy(step, distance).wait_send())
        for block in others:
            edge_copy(step, block).wait_send()


def shards(n_dom, adjoint, metric, base_flow, edge_list, flips):
    state_in = jnp.transpose(adjoint, (0, 2, 3, 1, 4)).reshape(3, NPTS, LOCAL, ELEMS)
    base_in = jnp.transpose(base_flow, (1, 0, 2))
    deriv = derivative_tables()
    span, fwd = span_tables()
    vmem = pl.BlockSpec(memory_space=pltpu.VMEM)
    dma = pltpu.SemaphoreType.DMA
    result = pl.pallas_call(
        functools.partial(kernel, n_dom),
        out_shape=jax.ShapeDtypeStruct((3, NPTS, LOCAL, ELEMS), F32),
        in_specs=[pl.BlockSpec(memory_space=pltpu.HBM)] * 8,
        out_specs=vmem,
        scratch_shapes=[
            pltpu.VMEM((3, KROWS, 128), F32),
            pltpu.VMEM((6, KROWS, 128), F32),
            pltpu.VMEM((12, STEPS, 128 * NPTS), F32),
            pltpu.VMEM((FLOWS * (NPTS + 2), 128), F32),
            pltpu.VMEM((FLOWS * MODES, 128), F32),
            pltpu.VMEM((FLOWS * MODES, 128), F32),
            pltpu.VMEM((STEPS, PLANE * WIRE, 128), F32),
            pltpu.VMEM((STEPS, PLANE * WIRE, 128), F32),
            pltpu.VMEM((STEPS, PLANE * BACK, 128), F32),
            pltpu.VMEM((STEPS, PLANE * BACK, 128), F32),
            pltpu.VMEM((STEPS, 128, 128), F32),
            pltpu.VMEM((STEPS, 128, 128), F32),
            pltpu.VMEM((3 * LOCAL * 16, 128), F32),
            pltpu.VMEM((128, 256), F32),
            pltpu.VMEM((128, 128), F32),
            pltpu.VMEM((128, 512), BF16),
            pltpu.VMEM((128, 256), BF16),
            pltpu.VMEM((KROWS, 128), F32),
            pltpu.VMEM((8, 128), F32),
            pltpu.VMEM((16, 128), jnp.int32),
            pltpu.VMEM((3, NPTS, LOCAL, ELEMS), F32),
            pltpu.VMEM((4, ELEMS), F32),
            pltpu.VMEM(deriv.shape, BF16),
            pltpu.VMEM((2 * REACH + 1, 1, CAP), jnp.int32),
            pltpu.VMEM((2 * REACH + 1, 1, CAP), jnp.int32),
            pltpu.VMEM(span.shape, BF16),
            pltpu.VMEM(fwd.shape, BF16),
            dma((8,)),
            dma((STEPS, PLANE - 1)),
            dma((STEPS, PLANE - 1)),
            dma((STEPS, PLANE - 1)),
            dma((STEPS, PLANE - 1)),
            dma((STEPS, 2 * REACH + 1)),
            dma((STEPS, 2 * REACH + 1)),
        ],
        compiler_params=pltpu.CompilerParams(
            collective_id=0, has_side_effects=True, vmem_limit_bytes=58 * 1024 * 1024
        ),
    )(
        state_in,
        metric,
        base_in,
        jnp.transpose(edge_list, (1, 0, 2)),
        jnp.transpose(flips, (1, 0, 2)),
        jnp.asarray(deriv),
        jnp.asarray(span),
        jnp.asarray(fwd),
    )
    return jnp.transpose(result.reshape(3, NODES, NODES, LOCAL, ELEMS), (0, 3, 1, 2, 4))


def solution(mesh):
    placed = (
        P(None, "plane", None, None, "dom"),
        P(None, "dom"),
        P(None, None, ("dom", "plane")),
        P("dom", None, None),
        P("dom", None, None),
    )
    return jax.shard_map(
        functools.partial(shards, mesh.shape["dom"]),
        mesh=mesh,
        in_specs=placed,
        out_specs=P(None, "plane", None, None, "dom"),
        check_vma=False,
    )
```

```python
import functools

import jax
import jax.numpy as jnp
import ml_dtypes
import numpy as np
from jax import lax
from jax.experimental import pallas as pl
from jax.experimental.pallas import tpu as pltpu
from jax.sharding import PartitionSpec as P

MODES = 64
STEPS = 2
NODES = 9
NPTS = NODES * NODES
ELEMS = 32
PLANE = 16
LOCAL = MODES // PLANE
SPAN_PTS = NPTS * ELEMS // PLANE
CAP = 24
REACH = 2
STEP_SIZE = 0.01
VISCOSITY = 0.02

ROWS = 88
KROWS = 96
WIRE = 48
BACK = 16
REST = SPAN_PTS - 128
FLOWS = 12 * STEPS

F32 = jnp.float32
BF16 = jnp.bfloat16
MESH_ID = pl.DeviceIdType.MESH


def split_table(table):
    hi = table.astype(np.float32).astype(ml_dtypes.bfloat16)
    lo = (table - hi.astype(np.float64)).astype(np.float32).astype(ml_dtypes.bfloat16)
    return np.concatenate([hi, hi, lo], axis=1)


def derivative_tables():
    order = NODES - 1
    ids = np.arange(NODES)
    coords = -np.cos(np.pi * ids / order)
    weight = np.where((ids == 0) | (ids == order), 2.0, 1.0)
    table = np.zeros((NODES, NODES))
    for a in range(NODES):
        for i in range(NODES):
            if a != i:
                table[a, i] = weight[a] / weight[i] * (-1.0) ** (a + i) / (coords[a] - coords[i])
    table -= np.diag(table.sum(axis=1))
    eye = np.eye(NODES)
    along_xi, along_eta = np.kron(table, eye), np.kron(eye, table)
    ops = [
        along_xi,
        along_eta,
        along_xi @ along_xi,
        along_xi @ along_eta,
        along_eta @ along_eta,
    ]
    stacked = np.zeros((len(ops) * ROWS, KROWS))
    for at, op in enumerate(ops):
        stacked[at * ROWS : at * ROWS + NPTS, :NPTS] = op
    return split_table(stacked)


def span_tables():
    modes = np.arange(MODES)
    wave = (modes + 1) // 2
    cosine = (modes % 2 == 1) | (modes == 0)
    angles = 2.0 * np.pi * ((np.arange(MODES)[:, None] * wave[None, :]) % MODES) / MODES
    basis = np.where(cosine[None, :], np.cos(angles), np.sin(angles))
    slope = np.where(cosine[None, :], -wave * np.sin(angles), wave * np.cos(angles))
    scale = np.where((modes == 0) | (modes == MODES - 1), 1.0 / MODES, 2.0 / MODES)
    forward = basis.T * scale[:, None]
    order = (np.arange(PLANE)[None, :] * LOCAL + np.arange(LOCAL)[:, None]).reshape(-1)
    span = np.concatenate([basis[:, order], slope[:, order]], axis=0)
    return split_table(span), split_table(forward[order])


def halves(x):
    hi = x.astype(BF16)
    return hi, (x - hi.astype(F32)).astype(BF16)


def three(x):
    hi, lo = halves(x)
    return jnp.concatenate([hi, lo, hi], axis=0)


def dot(a, b):
    return jnp.dot(a, b, preferred_element_type=F32)


def swap_blocks(parts):
    shape = parts[0].shape
    lane = lax.broadcasted_iota(jnp.int32, shape, 1)
    even = (lane // 32) % 2 == 0
    low = lane < 64
    a0, a1, a2, a3 = parts

    def near(x, y):
        return (
            jnp.where(even, x, pltpu.roll(y, 32, 1)),
            jnp.where(even, pltpu.roll(x, 96, 1), y),
        )

    def far(x, y):
        moved = pltpu.roll(jnp.where(low, y, x), 64, 1)
        return jnp.where(low, x, moved), jnp.where(low, moved, y)

    b0, b1 = near(a0, a1)
    b2, b3 = near(a2, a3)
    c0, c2 = far(b0, b2)
    c1, c3 = far(b1, b3)
    return [c0, c1, c2, c3]


def turn(x, shift):
    return pltpu.roll(x, shift % 128, 1) if shift % 128 else x


STATE_BLOCKS = 4
HEAD_AT = (0, 1, 2, 4, 5, 6, 7, 8, 9)
TAIL_AT = (3, 10, 11)
DISTANCES = (8, 7, 9, 6, 10, 5, 11, 4, 12, 3, 13, 2, 14, 1, 15)


def kernel(
    n_dom,
    adj_ref,
    met_ref,
    base_ref,
    edge_ref,
    flip_ref,
    deriv_ref,
    span_ref,
    fwd_ref,
    out_ref,
    state,
    grads,
    base_in,
    base_rows,
    base_head,
    base_tail,
    send_out,
    recv_out,
    send_back,
    recv_back,
    edge_out,
    edge_in,
    trace_a,
    trace_b,
    sums,
    send_hot,
    recv_hot,
    inv_weight,
    metrics,
    slot_ids,
    adj_in,
    met_in,
    deriv_in,
    edge_ids,
    flip_ids,
    span_in,
    fwd_in,
    load_sem,
    out_send,
    out_recv,
    back_send,
    back_recv,
    edge_send,
    edge_recv,
):
    dom = lax.axis_index("dom")
    me = lax.axis_index("plane")

    barrier = pltpu.get_barrier_semaphore()

    def greet(distance, carry):
        pl.semaphore_signal(
            barrier, inc=1, device_id=(dom, lax.rem(me + distance, PLANE)), device_id_type=MESH_ID
        )
        return carry

    lax.fori_loop(1, PLANE, greet, 0)
    others = [block for block in range(2 * REACH + 1) if block != REACH]
    for block in others:
        pl.semaphore_signal(
            barrier,
            inc=1,
            device_id=(lax.rem(dom + block - REACH + n_dom, n_dom), me),
            device_id_type=MESH_ID,
        )

    loads = {}
    for at, (name, source, target) in enumerate(
        (
            ("state", adj_ref, adj_in),
            ("metric", met_ref, met_in),
            ("deriv", deriv_ref, deriv_in),
            ("base", base_ref, base_in),
            ("edges", edge_ref, edge_ids),
            ("flips", flip_ref, flip_ids),
            ("span", span_ref, span_in),
            ("forward", fwd_ref, fwd_in),
        )
    ):
        loads[name] = pltpu.make_async_copy(source, target, load_sem.at[at])
        loads[name].start()

    def out_copy(step, distance):
        peer = lax.rem(me + distance, PLANE)
        return pltpu.make_async_remote_copy(
            src_ref=send_out.at[step, pl.ds(pl.multiple_of(peer * WIRE, 8), WIRE)],
            dst_ref=recv_out.at[step, pl.ds(pl.multiple_of(me * WIRE, 8), WIRE)],
            send_sem=out_send.at[step],
            recv_sem=out_recv.at[step],
            device_id=(dom, peer),
            device_id_type=MESH_ID,
        )

    def back_copy(step, distance):
        peer = lax.rem(me + distance, PLANE)
        return pltpu.make_async_remote_copy(
            src_ref=send_back.at[step, pl.ds(pl.multiple_of(peer * BACK, 8), BACK)],
            dst_ref=recv_back.at[step, pl.ds(pl.multiple_of(me * BACK, 8), BACK)],
            send_sem=back_send.at[step],
            recv_sem=back_recv.at[step],
            device_id=(dom, peer),
            device_id_type=MESH_ID,
        )

    def edge_copy(step, block):
        return pltpu.make_async_remote_copy(
            src_ref=edge_out.at[step, pl.ds(block * CAP, CAP)],
            dst_ref=edge_in.at[step, pl.ds((2 * REACH - block) * CAP, CAP)],
            send_sem=edge_send.at[step, block],
            recv_sem=edge_recv.at[step, block],
            device_id=(lax.rem(dom + block - REACH + n_dom, n_dom), me),
            device_id_type=MESH_ID,
        )

    def all_of(source, target, rows, send_sem, recv_sem, step):
        return pltpu.make_async_remote_copy(
            src_ref=source.at[step, pl.ds(0, (PLANE - 1) * rows)],
            dst_ref=target.at[step, pl.ds(0, (PLANE - 1) * rows)],
            send_sem=send_sem.at[step],
            recv_sem=recv_sem.at[step],
            device_id=(dom, lax.rem(me + 1, PLANE)),
            device_id_type=MESH_ID,
        )

    def each_peer(what):
        for distance in DISTANCES:
            what(distance)

    loads["state"].wait()
    for comp in range(3):
        for mode in range(LOCAL):
            state[comp, 0:NPTS, ELEMS * mode : ELEMS * (mode + 1)] = adj_in[comp, :, mode, :]
        state[comp, NPTS:KROWS, :] = jnp.zeros((KROWS - NPTS, 128), F32)
    loads["metric"].wait()
    for row in range(4):
        for group in range(4):
            metrics[row : row + 1, ELEMS * group : ELEMS * (group + 1)] = met_in[row : row + 1, :]
    xi_x, xi_y = metrics[0:1, :], metrics[1:2, :]
    eta_x, eta_y = metrics[2:3, :], metrics[3:4, :]

    lane_row = lax.broadcasted_iota(jnp.int32, (1, 128), 1)
    owner_lane = lax.broadcasted_iota(jnp.int32, (PLANE, 128), 1)
    owner_start = 2 * lax.broadcasted_iota(jnp.int32, (PLANE, 128), 0)
    after = owner_lane >= owner_start
    places = []
    for comp in range(3):
        place = (owner_lane - owner_start + (128 - REST * comp)) % 128
        places.append(place < REST)
    wave = ((LOCAL * me + lane_row // ELEMS + 1) // 2).astype(F32)

    def send_state(step):
        rhs = three(jnp.concatenate([state[0], state[1], state[2]], axis=1))
        if step == 0:
            loads["deriv"].wait()
        first = dot(deriv_in[0 : 2 * ROWS, :], rhs)
        for comp in range(3):
            lanes = slice(128 * comp, 128 * comp + 128)
            along_xi, along_eta = first[0:ROWS, lanes], first[ROWS : 2 * ROWS, lanes]
            grads[comp, 0:ROWS, :] = xi_x * along_xi + eta_x * along_eta
            grads[3 + comp, 0:ROWS, :] = xi_y * along_xi + eta_y * along_eta

        def nodes(field, k):
            rows = pl.ds(k, PLANE, stride=5)
            return state[field, rows, :] if field < 3 else grads[field - 3, rows, :]

        zeros = jnp.zeros((PLANE, 128), F32)

        def ends(first, second):
            parts = [nodes(first, 4), nodes(first, 5)]
            parts += [zeros, zeros] if second is None else [nodes(second, 4), nodes(second, 5)]
            return swap_blocks(parts)

        def put(at, mode, rows):
            send_out[step, pl.ds(at * 4 + mode, PLANE, stride=WIRE), :] = rows

        for group in range(3):
            fields = [3 * group + comp for comp in range(3)]
            early, late = ends(fields[0], fields[1]), ends(fields[2], None)
            packed = [zeros] * LOCAL
            for comp, field in enumerate(fields):
                heads = swap_blocks([nodes(field, k) for k in range(4)])
                both, side = (late, 0) if comp == 2 else (early, 64 * comp)
                for mode in range(LOCAL):
                    late_points = turn(both[mode], -side)
                    put(HEAD_AT[field], mode, jnp.where(after, heads[mode], late_points))
                    packed[mode] = jnp.where(
                        places[comp], turn(both[mode], REST * comp - side), packed[mode]
                    )
            for mode in range(LOCAL):
                put(TAIL_AT[group], mode, packed[mode])
        if step == 0:
            pl.semaphore_wait(barrier, PLANE - 1 + len(others))
        each_peer(lambda distance: out_copy(step, distance).start())
        mine = pl.ds(pl.multiple_of(me * WIRE, 8), WIRE)
        recv_out[step, mine, :] = send_out[step, mine, :]

        second = dot(deriv_in[2 * ROWS : 5 * ROWS, :], rhs)
        diffuse = STEP_SIZE * VISCOSITY
        keep = 1.0 - diffuse * (wave * wave)
        both_xi = diffuse * (xi_x * xi_x + xi_y * xi_y)
        mixed = (2.0 * diffuse) * (xi_x * eta_x + xi_y * eta_y)
        both_eta = diffuse * (eta_x * eta_x + eta_y * eta_y)
        for comp in range(3):
            lanes = slice(128 * comp, 128 * comp + 128)
            state[comp, 0:ROWS, :] = keep * state[comp, 0:ROWS, :] + (
                both_xi * second[0:ROWS, lanes]
                + mixed * second[ROWS : 2 * ROWS, lanes]
                + both_eta * second[2 * ROWS : 3 * ROWS, lanes]
            )

    def arrange_base():
        loads["base"].wait()

        def gather(block, carry):
            lanes = pl.ds(pl.multiple_of(128 * block, 128), 128)
            rows = pl.ds(pl.multiple_of(FLOWS * block, 8), FLOWS)
            base_rows[rows, :] = base_in[:, :, lanes].reshape(FLOWS, 128)
            return carry

        lax.fori_loop(0, NPTS, gather, 0)
        base_rows[FLOWS * NPTS :, :] = jnp.zeros((2 * FLOWS, 128), F32)
        lane = lax.broadcasted_iota(jnp.int32, (FLOWS, 128), 1)
        point = (lane - 2 * me + 128) % 128

        def body(n, carry):
            start = SPAN_PTS * n
            block = start // 128
            shift = start - 128 * block
            back = lax.rem(128 - shift + 2 * me, 128)
            early = point < 128 - shift
            rolled = []
            for at in range(3):
                rows = pl.ds(pl.multiple_of(FLOWS * (block + at), 8), FLOWS)
                rolled.append(pltpu.roll(base_rows[rows, :], back, 1))
            to = pl.ds(n, FLOWS, stride=MODES)
            base_head[to, :] = jnp.where(early, rolled[0], rolled[1])
            base_tail[to, :] = jnp.where(
                point < REST, jnp.where(early, rolled[1], rolled[2]), 0.0
            )
            return carry

        lax.fori_loop(0, MODES, body, 0)

    def prepare_edges():
        loads["edges"].wait()
        loads["flips"].wait()
        slot_ids[...] = jnp.full((16, 128), -1, jnp.int32)
        for block in range(2 * REACH + 1):
            lanes = slice(CAP * block, CAP * (block + 1))
            slot_ids[0:1, lanes] = edge_ids[block]
            slot_ids[8:9, lanes] = flip_ids[block]
        own, flip = slot_ids[0:1, :], slot_ids[8:9, :]
        odd = lane_row % 2 == 1
        paired = jnp.where(odd, pltpu.roll(own, 1, 1), pltpu.roll(own, 127, 1))
        inner = (lane_row >= CAP * REACH) & (lane_row < CAP * (REACH + 1))
        given = jnp.where(inner, paired, own)
        edge_row = lax.broadcasted_iota(jnp.int32, (128, 128), 0)
        hot = jnp.where(edge_row == own, 1.0, 0.0).astype(F32)
        recv_hot[:, 0:128] = hot.astype(BF16)
        recv_hot[:, 128:256] = hot.astype(BF16)
        gave = jnp.where(edge_row == given, 1.0, 0.0).astype(F32)
        turned = jnp.where(flip == 1, gave, 0.0)
        straight = (gave - turned).T.astype(BF16)
        turned = turned.T.astype(BF16)
        for part in range(2):
            send_hot[:, 256 * part : 256 * part + 128] = straight
            send_hot[:, 256 * part + 128 : 256 * part + 256] = turned
        counts = jnp.sum(hot.T, axis=0, keepdims=True)
        spread = []
        for edge in range(4):
            one = jnp.where(lane_row // ELEMS == edge, counts, 0.0)
            one = one + pltpu.roll(one, 64, 1)
            spread.append(one + pltpu.roll(one, 32, 1))
        inv_weight[...] = jnp.ones((KROWS, 128), F32)
        first_col, last_col = pl.ds(0, NODES, stride=NODES), pl.ds(8, NODES, stride=NODES)
        for rows, edge in ((first_col, 0), (slice(72, 81), 1), (last_col, 2), (slice(0, 9), 3)):
            inv_weight[rows, :] = inv_weight[rows, :] + spread[edge]
        inv_weight[...] = 1.0 / inv_weight[...]
        trace_b[...] = jnp.zeros((128, 256), F32)

    def physical(step):
        all_of(send_out, recv_out, WIRE, out_send, out_recv, step).wait_recv()
        columns = []
        for at in range(WIRE // LOCAL):
            columns.append(
                jnp.concatenate(
                    [
                        recv_out[step, pl.ds(at * 4 + mode, PLANE, stride=WIRE), :]
                        for mode in range(LOCAL)
                    ],
                    axis=0,
                )
            )
        state_rhs = three(jnp.concatenate(columns[:STATE_BLOCKS], axis=1))
        grad_rhs = three(jnp.concatenate(columns[STATE_BLOCKS:], axis=1))
        if step == 0:
            loads["span"].wait()
            loads["forward"].wait()
        of_state = dot(span_in[...], state_rhs)
        of_grads = dot(span_in[0:MODES, :], grad_rhs)

        def block_of(at, slope):
            if at < STATE_BLOCKS:
                rows = slice(MODES, 2 * MODES) if slope else slice(0, MODES)
                return of_state[rows, 128 * at : 128 * at + 128]
            at = at - STATE_BLOCKS
            return of_grads[:, 128 * at : 128 * at + 128]

        def head_of(field, slope=False):
            return block_of(HEAD_AT[field], slope)

        def tail_of(field, slope=False):
            packed = block_of(TAIL_AT[field // 3], slope)
            place = REST * (field % 3)
            return pltpu.roll(packed, 128 - place, 1) if place else packed

        def products(values, base):
            def flow(index):
                row = MODES * (STEPS * index + step)
                return base[row : row + MODES, :]

            state_now = [values(i) for i in range(3)]
            results = []
            for comp in range(3):
                term = (
                    flow(0) * values(3 + comp)
                    + flow(1) * values(6 + comp)
                    + flow(2) * values(comp, True)
                )
                results.append(
                    term
                    - (
                        state_now[0] * flow(3 + comp)
                        + state_now[1] * flow(6 + comp)
                        + state_now[2] * flow(9 + comp)
                    )
                )
            return results

        heads = products(head_of, base_head)
        tails = products(tail_of, base_tail)
        rest = tails[0] + pltpu.roll(tails[1], REST, 1) + pltpu.roll(tails[2], 2 * REST, 1)
        packed = heads + [rest]
        back = dot(fwd_in[...], three(jnp.concatenate(packed, axis=1)))
        for at in range(4):
            for mode in range(LOCAL):
                send_back[step, pl.ds(at * 4 + mode, PLANE, stride=BACK), :] = back[
                    PLANE * mode : PLANE * (mode + 1), 128 * at : 128 * at + 128
                ]
        each_peer(lambda distance: back_copy(step, distance).start())
        mine = pl.ds(pl.multiple_of(me * BACK, 8), BACK)
        recv_back[step, mine, :] = send_back[step, mine, :]

    def update(step):
        all_of(send_back, recv_back, BACK, back_send, back_recv, step).wait_recv()
        def came(at, mode):
            return recv_back[step, pl.ds(at * 4 + mode, PLANE, stride=BACK), :]

        rest = [came(3, mode) for mode in range(LOCAL)]
        heads, ends = [], []
        for comp in range(3):
            firsts, lasts = [], []
            for mode in range(LOCAL):
                moved = came(comp, mode)
                last = jnp.where(places[0], turn(rest[mode], -REST * comp), 0.0)
                firsts.append(jnp.where(after, moved, 0.0))
                lasts.append(jnp.where(after, last, moved))
            heads.append(swap_blocks(firsts))
            ends.append(lasts)
        joined = [jnp.where(owner_lane < 64, x, pltpu.roll(y, 64, 1)) for x, y in zip(*ends[:2])]
        early, late = swap_blocks(joined), swap_blocks(ends[2])
        ends = (early[:2], early[2:], late[:2])
        for comp in range(3):
            for k, rate in enumerate(heads[comp] + ends[comp]):
                rows = pl.ds(k, PLANE, stride=5)
                state[comp, rows, :] = state[comp, rows, :] + STEP_SIZE * rate

    def exchange(step):
        first_col, last_col = pl.ds(0, NODES, stride=NODES), pl.ds(8, NODES, stride=NODES)
        edge_rows = (first_col, slice(72, 81), last_col, slice(0, 9))
        for comp in range(3):
            traces = swap_blocks([state[comp, rows, :] for rows in edge_rows])
            for mode in range(LOCAL):
                at = (comp * LOCAL + mode) * 16
                trace_a[at : at + NODES, :] = traces[mode]
        for i in range(NODES):
            rows = trace_a[pl.ds(i, 3 * LOCAL, stride=16), :]
            trace_b[12 * i : 12 * i + 12, 0:128] = rows
            trace_b[12 * (8 - i) : 12 * (8 - i) + 12, 128:256] = rows
        hi, lo = halves(trace_b[...])
        given = lax.dot_general(
            send_hot[...],
            jnp.concatenate([hi, lo], axis=1),
            (((1,), (1,)), ((), ())),
            preferred_element_type=F32,
        )
        edge_out[step] = given
        for block in others:
            edge_copy(step, block).start()
        inner = slice(CAP * REACH, CAP * (REACH + 1))
        edge_in[step, inner, :] = given[inner, :]
        edge_in[step, 120:128, :] = jnp.zeros((8, 128), F32)
        for block in others:
            edge_copy(step, block).wait_recv()
        hi, lo = halves(edge_in[step])
        sums[...] = dot(recv_hot[...], jnp.concatenate([hi, lo], axis=0)).T
        for comp in range(3):
            parts = swap_blocks(
                [sums[pl.ds(comp * LOCAL + mode, NODES, stride=12), :] for mode in range(LOCAL)]
            )
            for rows, part in zip(edge_rows, parts):
                state[comp, rows, :] = state[comp, rows, :] + part
            state[comp, 0:ROWS, :] = state[comp, 0:ROWS, :] * inv_weight[0:ROWS, :]

    for step in range(STEPS):
        send_state(step)
        if step == 0:
            prepare_edges()
            arrange_base()
        physical(step)
        update(step)
        exchange(step)

    out_ref[...] = state[...]

    for step in range(STEPS):
        all_of(send_out, recv_out, WIRE, out_send, out_recv, step).wait_send()
        all_of(send_back, recv_back, BACK, back_send, back_recv, step).wait_send()
        for block in others:
            edge_copy(step, block).wait_send()


def lay_out(state, out_ref):
    for comp in range(3):
        for mode in range(LOCAL):
            out_ref[comp, :, mode, :] = state[comp, 0:NPTS, ELEMS * mode : ELEMS * (mode + 1)]


def shards(n_dom, adjoint, metric, base_flow, edge_list, flips):
    state_in = jnp.transpose(adjoint, (0, 2, 3, 1, 4)).reshape(3, NPTS, LOCAL, ELEMS)
    base_in = jnp.transpose(base_flow, (1, 0, 2))
    deriv = derivative_tables()
    span, fwd = span_tables()
    vmem = pl.BlockSpec(memory_space=pltpu.VMEM)
    dma = pltpu.SemaphoreType.DMA
    result = pl.pallas_call(
        functools.partial(kernel, n_dom),
        out_shape=jax.ShapeDtypeStruct((3, KROWS, 128), F32),
        in_specs=[pl.BlockSpec(memory_space=pltpu.HBM)] * 8,
        out_specs=vmem,
        scratch_shapes=[
            pltpu.VMEM((3, KROWS, 128), F32),
            pltpu.VMEM((6, KROWS, 128), F32),
            pltpu.VMEM((12, STEPS, 128 * NPTS), F32),
            pltpu.VMEM((FLOWS * (NPTS + 2), 128), F32),
            pltpu.VMEM((FLOWS * MODES, 128), F32),
            pltpu.VMEM((FLOWS * MODES, 128), F32),
            pltpu.VMEM((STEPS, PLANE * WIRE, 128), F32),
            pltpu.VMEM((STEPS, PLANE * WIRE, 128), F32),
            pltpu.VMEM((STEPS, PLANE * BACK, 128), F32),
            pltpu.VMEM((STEPS, PLANE * BACK, 128), F32),
            pltpu.VMEM((STEPS, 128, 128), F32),
            pltpu.VMEM((STEPS, 128, 128), F32),
            pltpu.VMEM((3 * LOCAL * 16, 128), F32),
            pltpu.VMEM((128, 256), F32),
            pltpu.VMEM((128, 128), F32),
            pltpu.VMEM((128, 512), BF16),
            pltpu.VMEM((128, 256), BF16),
            pltpu.VMEM((KROWS, 128), F32),
            pltpu.VMEM((8, 128), F32),
            pltpu.VMEM((16, 128), jnp.int32),
            pltpu.VMEM((3, NPTS, LOCAL, ELEMS), F32),
            pltpu.VMEM((4, ELEMS), F32),
            pltpu.VMEM(deriv.shape, BF16),
            pltpu.VMEM((2 * REACH + 1, 1, CAP), jnp.int32),
            pltpu.VMEM((2 * REACH + 1, 1, CAP), jnp.int32),
            pltpu.VMEM(span.shape, BF16),
            pltpu.VMEM(fwd.shape, BF16),
            dma((8,)),
            dma((STEPS,)),
            dma((STEPS,)),
            dma((STEPS,)),
            dma((STEPS,)),
            dma((STEPS, 2 * REACH + 1)),
            dma((STEPS, 2 * REACH + 1)),
        ],
        compiler_params=pltpu.CompilerParams(
            collective_id=0, has_side_effects=True, vmem_limit_bytes=58 * 1024 * 1024
        ),
    )(
        state_in,
        metric,
        base_in,
        jnp.transpose(edge_list, (1, 0, 2)),
        jnp.transpose(flips, (1, 0, 2)),
        jnp.asarray(deriv),
        jnp.asarray(span),
        jnp.asarray(fwd),
    )
    result = pl.pallas_call(
        lay_out,
        out_shape=jax.ShapeDtypeStruct((3, NPTS, LOCAL, ELEMS), F32),
        in_specs=[vmem],
        out_specs=vmem,
    )(result)
    return jnp.transpose(result.reshape(3, NODES, NODES, LOCAL, ELEMS), (0, 3, 1, 2, 4))


def solution(mesh):
    placed = (
        P(None, "plane", None, None, "dom"),
        P(None, "dom"),
        P(None, None, ("dom", "plane")),
        P("dom", None, None),
        P("dom", None, None),
    )
    return jax.shard_map(
        functools.partial(shards, mesh.shape["dom"]),
        mesh=mesh,
        in_specs=placed,
        out_specs=P(None, "plane", None, None, "dom"),
        check_vma=False,
    )
```

```python
import functools

import jax
import jax.numpy as jnp
import ml_dtypes
import numpy as np
from jax import lax
from jax.experimental import pallas as pl
from jax.experimental.pallas import tpu as pltpu
from jax.sharding import PartitionSpec as P

MODES = 64
STEPS = 2
NODES = 9
NPTS = NODES * NODES
ELEMS = 32
PLANE = 16
LOCAL = MODES // PLANE
SPAN_PTS = NPTS * ELEMS // PLANE
CAP = 24
REACH = 2
STEP_SIZE = 0.01
VISCOSITY = 0.02

ROWS = 88
KROWS = 96
WIRE = 48
BACK = 8
REST = SPAN_PTS - 128
FLOWS = 12 * STEPS

F32 = jnp.float32
BF16 = jnp.bfloat16
MESH_ID = pl.DeviceIdType.MESH


def split_table(table):
    hi = table.astype(np.float32).astype(ml_dtypes.bfloat16)
    lo = (table - hi.astype(np.float64)).astype(np.float32).astype(ml_dtypes.bfloat16)
    return np.concatenate([hi, hi, lo], axis=1)


def derivative_tables():
    order = NODES - 1
    ids = np.arange(NODES)
    coords = -np.cos(np.pi * ids / order)
    weight = np.where((ids == 0) | (ids == order), 2.0, 1.0)
    table = np.zeros((NODES, NODES))
    for a in range(NODES):
        for i in range(NODES):
            if a != i:
                table[a, i] = weight[a] / weight[i] * (-1.0) ** (a + i) / (coords[a] - coords[i])
    table -= np.diag(table.sum(axis=1))
    eye = np.eye(NODES)
    along_xi, along_eta = np.kron(table, eye), np.kron(eye, table)
    ops = [
        along_xi,
        along_eta,
        along_xi @ along_xi,
        along_xi @ along_eta,
        along_eta @ along_eta,
    ]
    stacked = np.zeros((len(ops) * ROWS, KROWS))
    for at, op in enumerate(ops):
        stacked[at * ROWS : at * ROWS + NPTS, :NPTS] = op
    return split_table(stacked)


def span_tables():
    modes = np.arange(MODES)
    wave = (modes + 1) // 2
    cosine = (modes % 2 == 1) | (modes == 0)
    angles = 2.0 * np.pi * ((np.arange(MODES)[:, None] * wave[None, :]) % MODES) / MODES
    basis = np.where(cosine[None, :], np.cos(angles), np.sin(angles))
    slope = np.where(cosine[None, :], -wave * np.sin(angles), wave * np.cos(angles))
    scale = np.where((modes == 0) | (modes == MODES - 1), 1.0 / MODES, 2.0 / MODES)
    forward = basis.T * scale[:, None]
    order = (np.arange(PLANE)[None, :] * LOCAL + np.arange(LOCAL)[:, None]).reshape(-1)
    span = np.concatenate([basis[:, order], slope[:, order]], axis=0)
    return split_table(span), split_table(forward[order])


def halves(x):
    hi = x.astype(BF16)
    return hi, (x - hi.astype(F32)).astype(BF16)


def three(x):
    hi, lo = halves(x)
    return jnp.concatenate([hi, lo, hi], axis=0)


def dot(a, b):
    return jnp.dot(a, b, preferred_element_type=F32)


def swap_blocks(parts):
    shape = parts[0].shape
    lane = lax.broadcasted_iota(jnp.int32, shape, 1)
    even = (lane // 32) % 2 == 0
    low = lane < 64
    a0, a1, a2, a3 = parts

    def near(x, y):
        return (
            jnp.where(even, x, pltpu.roll(y, 32, 1)),
            jnp.where(even, pltpu.roll(x, 96, 1), y),
        )

    def far(x, y):
        moved = pltpu.roll(jnp.where(low, y, x), 64, 1)
        return jnp.where(low, x, moved), jnp.where(low, moved, y)

    b0, b1 = near(a0, a1)
    b2, b3 = near(a2, a3)
    c0, c2 = far(b0, b2)
    c1, c3 = far(b1, b3)
    return [c0, c1, c2, c3]


def turn(x, shift):
    return pltpu.roll(x, shift % 128, 1) if shift % 128 else x


STATE_AT = ((0, 8, 16), (0, 16, 32))
GRAD_AT = ((24, 32, 40), (8, 24, 40))
CHUNKS = (((0, 24), (24, 8), (32, 8), (40, 8)), ((0, 16), (16, 16), (32, 8), (40, 8)))
DISTANCES = (8, 7, 9, 6, 10, 5, 11, 4, 12, 3, 13, 2, 14, 1, 15)


def kernel(
    n_dom,
    adj_ref,
    met_ref,
    base_ref,
    edge_ref,
    flip_ref,
    deriv_ref,
    span_ref,
    fwd_ref,
    out_ref,
    state,
    grads,
    base_in,
    base_rows,
    base_head,
    base_tail,
    send_out,
    recv_out,
    send_back,
    recv_back,
    edge_out,
    edge_in,
    trace_a,
    trace_b,
    sums,
    send_hot,
    recv_hot,
    inv_weight,
    metrics,
    slot_ids,
    adj_in,
    met_in,
    deriv_in,
    edge_ids,
    flip_ids,
    span_in,
    fwd_in,
    load_sem,
    out_send,
    out_recv,
    back_send,
    back_recv,
    edge_send,
    edge_recv,
):
    dom = lax.axis_index("dom")
    me = lax.axis_index("plane")

    barrier = pltpu.get_barrier_semaphore()

    def greet(distance, carry):
        pl.semaphore_signal(
            barrier, inc=1, device_id=(dom, lax.rem(me + distance, PLANE)), device_id_type=MESH_ID
        )
        return carry

    lax.fori_loop(1, PLANE, greet, 0)
    others = [block for block in range(2 * REACH + 1) if block != REACH]
    for block in others:
        pl.semaphore_signal(
            barrier,
            inc=1,
            device_id=(lax.rem(dom + block - REACH + n_dom, n_dom), me),
            device_id_type=MESH_ID,
        )

    loads = {}
    for at, (name, source, target) in enumerate(
        (
            ("state", adj_ref, adj_in),
            ("metric", met_ref, met_in),
            ("deriv", deriv_ref, deriv_in),
            ("base", base_ref, base_in),
            ("edges", edge_ref, edge_ids),
            ("flips", flip_ref, flip_ids),
            ("span", span_ref, span_in),
            ("forward", fwd_ref, fwd_in),
        )
    ):
        loads[name] = pltpu.make_async_copy(source, target, load_sem.at[at])
        loads[name].start()

    def out_copy(step, chunk, distance):
        peer = lax.rem(me + distance, PLANE)
        start, rows = CHUNKS[step][chunk]
        return pltpu.make_async_remote_copy(
            src_ref=send_out.at[step, pl.ds(pl.multiple_of(peer * WIRE + start, 8), rows)],
            dst_ref=recv_out.at[step, pl.ds(pl.multiple_of(me * WIRE + start, 8), rows)],
            send_sem=out_send.at[step, chunk],
            recv_sem=out_recv.at[step, chunk],
            device_id=(dom, peer),
            device_id_type=MESH_ID,
        )

    def back_copy(step, comp, distance):
        peer = lax.rem(me + distance, PLANE)
        return pltpu.make_async_remote_copy(
            src_ref=send_back.at[step, comp, pl.ds(pl.multiple_of(peer * BACK, 8), BACK)],
            dst_ref=recv_back.at[step, comp, pl.ds(pl.multiple_of(me * BACK, 8), BACK)],
            send_sem=back_send.at[step, comp],
            recv_sem=back_recv.at[step, comp],
            device_id=(dom, peer),
            device_id_type=MESH_ID,
        )

    def edge_copy(step, comp, block):
        return pltpu.make_async_remote_copy(
            src_ref=edge_out.at[step, comp, pl.ds(block * CAP, CAP)],
            dst_ref=edge_in.at[step, comp, pl.ds((2 * REACH - block) * CAP, CAP)],
            send_sem=edge_send.at[step, comp],
            recv_sem=edge_recv.at[step, comp],
            device_id=(lax.rem(dom + block - REACH + n_dom, n_dom), me),
            device_id_type=MESH_ID,
        )

    def all_of(source, target, rows, send_sem, recv_sem):
        return pltpu.make_async_remote_copy(
            src_ref=source.at[pl.ds(0, rows)],
            dst_ref=target.at[pl.ds(0, rows)],
            send_sem=send_sem,
            recv_sem=recv_sem,
            device_id=(dom, lax.rem(me + 1, PLANE)),
            device_id_type=MESH_ID,
        )

    def all_out(step, chunk):
        rows = (PLANE - 1) * CHUNKS[step][chunk][1]
        sems = out_send.at[step, chunk], out_recv.at[step, chunk]
        return all_of(send_out.at[step], recv_out.at[step], rows, *sems)

    def all_back(step, comp):
        rows = (PLANE - 1) * BACK
        sems = back_send.at[step, comp], back_recv.at[step, comp]
        return all_of(send_back.at[step, comp], recv_back.at[step, comp], rows, *sems)

    def all_edges(step, comp):
        sems = edge_send.at[step, comp], edge_recv.at[step, comp]
        return all_of(edge_out.at[step, comp], edge_in.at[step, comp], 2 * REACH * CAP, *sems)

    def each_peer(what):
        for distance in DISTANCES:
            what(distance)

    loads["state"].wait()
    for comp in range(3):
        for mode in range(LOCAL):
            state[comp, 0:NPTS, ELEMS * mode : ELEMS * (mode + 1)] = adj_in[comp, :, mode, :]
        state[comp, NPTS:KROWS, :] = jnp.zeros((KROWS - NPTS, 128), F32)
    loads["metric"].wait()
    for row in range(4):
        for group in range(4):
            metrics[row : row + 1, ELEMS * group : ELEMS * (group + 1)] = met_in[row : row + 1, :]
    xi_x, xi_y = metrics[0:1, :], metrics[1:2, :]
    eta_x, eta_y = metrics[2:3, :], metrics[3:4, :]

    lane_row = lax.broadcasted_iota(jnp.int32, (1, 128), 1)
    owner_lane = lax.broadcasted_iota(jnp.int32, (PLANE, 128), 1)
    owner_start = 2 * lax.broadcasted_iota(jnp.int32, (PLANE, 128), 0)
    after = owner_lane >= owner_start
    places = []
    for comp in range(3):
        place = (owner_lane - owner_start + (128 - REST * comp)) % 128
        places.append(place < REST)
    wave = ((LOCAL * me + lane_row // ELEMS + 1) // 2).astype(F32)

    def split_state(comp):
        return three(state[comp])

    def derive(step, comp, rhs):
        first = dot(deriv_in[0 : 2 * ROWS, :], rhs)
        along_xi, along_eta = first[0:ROWS, :], first[ROWS : 2 * ROWS, :]
        grads[2 * comp, 0:ROWS, :] = xi_x * along_xi + eta_x * along_eta
        grads[2 * comp + 1, 0:ROWS, :] = xi_y * along_xi + eta_y * along_eta

        def nodes(field, k):
            rows = pl.ds(k, PLANE, stride=5)
            return grads[2 * comp + field - 1, rows, :] if field else state[comp, rows, :]

        zeros = jnp.zeros((PLANE, 128), F32)

        def put(at, mode, rows):
            send_out[step, pl.ds(at + mode, PLANE, stride=WIRE), :] = rows

        early = swap_blocks([nodes(0, 4), nodes(0, 5), nodes(1, 4), nodes(1, 5)])
        late = swap_blocks([nodes(2, 4), nodes(2, 5), zeros, zeros])
        packed = [zeros] * LOCAL
        to = (STATE_AT[step][comp], GRAD_AT[step][comp], GRAD_AT[step][comp] + LOCAL)
        for field in range(3):
            heads = swap_blocks([nodes(field, k) for k in range(4)])
            both, side = (late, 0) if field == 2 else (early, 64 * field)
            for mode in range(LOCAL):
                put(to[field], mode, jnp.where(after, heads[mode], turn(both[mode], -side)))
                packed[mode] = jnp.where(
                    places[field], turn(both[mode], REST * field - side), packed[mode]
                )
        for mode in range(LOCAL):
            put(STATE_AT[step][comp] + LOCAL, mode, packed[mode])

    def send_chunk(step, chunk):
        each_peer(lambda distance: out_copy(step, chunk, distance).start())

    def keep_chunk(step, chunk):
        start, rows = CHUNKS[step][chunk]
        mine = pl.ds(pl.multiple_of(me * WIRE + start, 8), rows)
        recv_out[step, mine, :] = send_out[step, mine, :]

    def diffuse(comp, rhs):
        second = dot(deriv_in[2 * ROWS : 5 * ROWS, :], rhs)
        factor = STEP_SIZE * VISCOSITY
        keep = 1.0 - factor * (wave * wave)
        both_xi = factor * (xi_x * xi_x + xi_y * xi_y)
        mixed = (2.0 * factor) * (xi_x * eta_x + xi_y * eta_y)
        both_eta = factor * (eta_x * eta_x + eta_y * eta_y)
        state[comp, 0:ROWS, :] = keep * state[comp, 0:ROWS, :] + (
            both_xi * second[0:ROWS, :]
            + mixed * second[ROWS : 2 * ROWS, :]
            + both_eta * second[2 * ROWS : 3 * ROWS, :]
        )

    def gather_base():
        loads["base"].wait()

        def gather(block, carry):
            lanes = pl.ds(pl.multiple_of(128 * block, 128), 128)
            rows = pl.ds(pl.multiple_of(FLOWS * block, 8), FLOWS)
            base_rows[rows, :] = base_in[:, :, lanes].reshape(FLOWS, 128)
            return carry

        lax.fori_loop(0, NPTS, gather, 0)
        base_rows[FLOWS * NPTS :, :] = jnp.zeros((2 * FLOWS, 128), F32)

    def arrange_base():
        lane = lax.broadcasted_iota(jnp.int32, (FLOWS, 128), 1)
        point = (lane - 2 * me + 128) % 128

        def body(n, carry):
            start = SPAN_PTS * n
            block = start // 128
            shift = start - 128 * block
            back = lax.rem(128 - shift + 2 * me, 128)
            early = point < 128 - shift
            rolled = []
            for at in range(3):
                rows = pl.ds(pl.multiple_of(FLOWS * (block + at), 8), FLOWS)
                rolled.append(pltpu.roll(base_rows[rows, :], back, 1))
            to = pl.ds(n, FLOWS, stride=MODES)
            base_head[to, :] = jnp.where(early, rolled[0], rolled[1])
            base_tail[to, :] = jnp.where(
                point < REST, jnp.where(early, rolled[1], rolled[2]), 0.0
            )
            return carry

        lax.fori_loop(0, MODES, body, 0)

    def prepare_edges():
        loads["edges"].wait()
        loads["flips"].wait()
        slot_ids[...] = jnp.full((16, 128), -1, jnp.int32)
        for block in range(2 * REACH + 1):
            lanes = slice(CAP * block, CAP * (block + 1))
            slot_ids[0:1, lanes] = edge_ids[block]
            slot_ids[8:9, lanes] = flip_ids[block]
        own, flip = slot_ids[0:1, :], slot_ids[8:9, :]
        odd = lane_row % 2 == 1
        paired = jnp.where(odd, pltpu.roll(own, 1, 1), pltpu.roll(own, 127, 1))
        inner = (lane_row >= CAP * REACH) & (lane_row < CAP * (REACH + 1))
        given = jnp.where(inner, paired, own)
        edge_row = lax.broadcasted_iota(jnp.int32, (128, 128), 0)
        hot = jnp.where(edge_row == own, 1.0, 0.0).astype(F32)
        recv_hot[:, 0:128] = hot.astype(BF16)
        recv_hot[:, 128:256] = hot.astype(BF16)
        gave = jnp.where(edge_row == given, 1.0, 0.0).astype(F32)
        turned = jnp.where(flip == 1, gave, 0.0)
        straight = (gave - turned).T.astype(BF16)
        turned = turned.T.astype(BF16)
        for part in range(2):
            send_hot[:, 256 * part : 256 * part + 128] = straight
            send_hot[:, 256 * part + 128 : 256 * part + 256] = turned
        counts = jnp.sum(hot.T, axis=0, keepdims=True)
        spread = []
        for edge in range(4):
            one = jnp.where(lane_row // ELEMS == edge, counts, 0.0)
            one = one + pltpu.roll(one, 64, 1)
            spread.append(one + pltpu.roll(one, 32, 1))
        inv_weight[...] = jnp.ones((KROWS, 128), F32)
        for edge, rows in enumerate(edge_rows):
            inv_weight[rows, :] = inv_weight[rows, :] + spread[edge]
        inv_weight[...] = 1.0 / inv_weight[...]
        trace_b[...] = jnp.zeros((128, 256), F32)

    def physical(step):
        def column(at):
            return jnp.concatenate(
                [
                    recv_out[step, pl.ds(at + mode, PLANE, stride=WIRE), :]
                    for mode in range(LOCAL)
                ],
                axis=0,
            )

        for chunk in range(1 if step == 0 else 3):
            all_out(step, chunk).wait_recv()
        columns = []
        for comp in range(3):
            columns += [column(STATE_AT[step][comp]), column(STATE_AT[step][comp] + LOCAL)]
        of_state = dot(span_in[...], three(jnp.concatenate(columns, axis=1)))

        def flow(base, index):
            row = MODES * (STEPS * index + step)
            return base[row : row + MODES, :]

        def product(comp, base, side, along_x, along_y):
            def now(i, slope=False):
                lanes = 128 * (2 * i + side)
                rows = slice(MODES, 2 * MODES) if slope else slice(0, MODES)
                return of_state[rows, lanes : lanes + 128]

            term = (
                flow(base, 0) * along_x + flow(base, 1) * along_y + flow(base, 2) * now(comp, True)
            )
            return term - (
                now(0) * flow(base, 3 + comp)
                + now(1) * flow(base, 6 + comp)
                + now(2) * flow(base, 9 + comp)
            )

        for comp in range(3):
            if step == 0 or comp == 2:
                all_out(step, comp + 1).wait_recv()
            at = GRAD_AT[step][comp]
            rhs = three(jnp.concatenate([column(at), column(at + LOCAL)], axis=1))
            of_grads = dot(span_in[0:MODES, :], rhs)
            first = product(comp, base_head, 0, of_grads[:, 0:128], of_grads[:, 128:256])
            rest_now = of_state[0:MODES, 128 * (2 * comp + 1) : 128 * (2 * comp + 2)]
            rest = product(comp, base_tail, 1, turn(rest_now, -REST), turn(rest_now, -2 * REST))
            back = dot(fwd_in[...], three(jnp.concatenate([first, rest], axis=1)))
            for at in range(2):
                for mode in range(LOCAL):
                    send_back[step, comp, pl.ds(at * LOCAL + mode, PLANE, stride=BACK), :] = back[
                        PLANE * mode : PLANE * (mode + 1), 128 * at : 128 * at + 128
                    ]
            each_peer(lambda distance, comp=comp: back_copy(step, comp, distance).start())
            mine = pl.ds(pl.multiple_of(me * BACK, 8), BACK)
            recv_back[step, comp, mine, :] = send_back[step, comp, mine, :]

    first_col, last_col = pl.ds(0, NODES, stride=NODES), pl.ds(8, NODES, stride=NODES)
    edge_rows = (first_col, slice(72, 81), last_col, slice(0, 9))

    def update(step, comp):
        all_back(step, comp).wait_recv()

        def came(at):
            return recv_back[step, comp, pl.ds(at, PLANE, stride=BACK), :]

        firsts, lasts = [], []
        for mode in range(LOCAL):
            moved = came(mode)
            last = jnp.where(places[0], came(LOCAL + mode), 0.0)
            firsts.append(jnp.where(after, moved, 0.0))
            lasts.append(jnp.where(after, last, moved))
        for k, rate in enumerate(swap_blocks(firsts) + swap_blocks(lasts)[:2]):
            rows = pl.ds(k, PLANE, stride=5)
            state[comp, rows, :] = state[comp, rows, :] + STEP_SIZE * rate

    def give_edges(step, comp):
        traces = swap_blocks([state[comp, rows, :] for rows in edge_rows])
        for mode in range(LOCAL):
            trace_a[mode * 16 : mode * 16 + NODES, :] = traces[mode]
        for i in range(NODES):
            rows = trace_a[pl.ds(i, LOCAL, stride=16), :]
            trace_b[LOCAL * i : LOCAL * (i + 1), 0:128] = rows
            trace_b[LOCAL * (8 - i) : LOCAL * (9 - i), 128:256] = rows
        hi, lo = halves(trace_b[...])
        given = lax.dot_general(
            send_hot[...],
            jnp.concatenate([hi, lo], axis=1),
            (((1,), (1,)), ((), ())),
            preferred_element_type=F32,
        )
        edge_out[step, comp] = given
        for block in others:
            edge_copy(step, comp, block).start()
        inner = slice(CAP * REACH, CAP * (REACH + 1))
        edge_in[step, comp, inner, :] = given[inner, :]
        edge_in[step, comp, 120:128, :] = jnp.zeros((8, 128), F32)

    def take_edges(step, comp):
        all_edges(step, comp).wait_recv()
        hi, lo = halves(edge_in[step, comp])
        sums[...] = dot(recv_hot[...], jnp.concatenate([hi, lo], axis=0)).T
        parts = swap_blocks([sums[pl.ds(mode, NODES, stride=LOCAL), :] for mode in range(LOCAL)])
        for rows, part in zip(edge_rows, parts):
            state[comp, rows, :] = state[comp, rows, :] + part
        state[comp, 0:ROWS, :] = state[comp, 0:ROWS, :] * inv_weight[0:ROWS, :]

    loads["deriv"].wait()
    halved = [split_state(comp) for comp in range(3)]
    for comp in range(3):
        derive(0, comp, halved[comp])
    prepare_edges()
    gather_base()
    pl.semaphore_wait(barrier, PLANE - 1 + len(others))
    for chunk in range(4):
        send_chunk(0, chunk)
    for chunk in range(4):
        keep_chunk(0, chunk)
    for comp in range(3):
        diffuse(comp, halved[comp])
    arrange_base()
    loads["span"].wait()
    loads["forward"].wait()
    physical(0)
    for comp in range(3):
        update(0, comp)
        give_edges(0, comp)
    halved = []
    for comp in range(3):
        take_edges(0, comp)
        halved.append(split_state(comp))
        derive(1, comp, halved[comp])
        for chunk in (comp,) if comp < 2 else (2, 3):
            send_chunk(1, chunk)
    for chunk in range(4):
        keep_chunk(1, chunk)
    for comp in range(3):
        diffuse(comp, halved[comp])
    physical(1)
    for comp in range(3):
        update(1, comp)
        give_edges(1, comp)
    for comp in range(3):
        take_edges(1, comp)
        out_ref[comp] = state[comp, 0:NPTS, :]

    for step in range(STEPS):
        for chunk in range(4):
            all_out(step, chunk).wait_send()
        for comp in range(3):
            all_back(step, comp).wait_send()
            all_edges(step, comp).wait_send()


def shards(n_dom, adjoint, metric, base_flow, edge_list, flips):
    state_in = jnp.transpose(adjoint, (0, 2, 3, 1, 4)).reshape(3, NPTS, LOCAL, ELEMS)
    base_in = jnp.transpose(base_flow, (1, 0, 2))
    deriv = derivative_tables()
    span, fwd = span_tables()
    vmem = pl.BlockSpec(memory_space=pltpu.VMEM)
    dma = pltpu.SemaphoreType.DMA
    result = pl.pallas_call(
        functools.partial(kernel, n_dom),
        out_shape=jax.ShapeDtypeStruct((3, NPTS, 128), F32),
        in_specs=[pl.BlockSpec(memory_space=pltpu.HBM)] * 8,
        out_specs=vmem,
        scratch_shapes=[
            pltpu.VMEM((3, KROWS, 128), F32),
            pltpu.VMEM((6, KROWS, 128), F32),
            pltpu.VMEM((12, STEPS, 128 * NPTS), F32),
            pltpu.VMEM((FLOWS * (NPTS + 2), 128), F32),
            pltpu.VMEM((FLOWS * MODES, 128), F32),
            pltpu.VMEM((FLOWS * MODES, 128), F32),
            pltpu.VMEM((STEPS, PLANE * WIRE, 128), F32),
            pltpu.VMEM((STEPS, PLANE * WIRE, 128), F32),
            pltpu.VMEM((STEPS, 3, PLANE * BACK, 128), F32),
            pltpu.VMEM((STEPS, 3, PLANE * BACK, 128), F32),
            pltpu.VMEM((STEPS, 3, 128, 128), F32),
            pltpu.VMEM((STEPS, 3, 128, 128), F32),
            pltpu.VMEM((LOCAL * 16, 128), F32),
            pltpu.VMEM((128, 256), F32),
            pltpu.VMEM((128, 128), F32),
            pltpu.VMEM((128, 512), BF16),
            pltpu.VMEM((128, 256), BF16),
            pltpu.VMEM((KROWS, 128), F32),
            pltpu.VMEM((8, 128), F32),
            pltpu.VMEM((16, 128), jnp.int32),
            pltpu.VMEM((3, NPTS, LOCAL, ELEMS), F32),
            pltpu.VMEM((4, ELEMS), F32),
            pltpu.VMEM(deriv.shape, BF16),
            pltpu.VMEM((2 * REACH + 1, 1, CAP), jnp.int32),
            pltpu.VMEM((2 * REACH + 1, 1, CAP), jnp.int32),
            pltpu.VMEM(span.shape, BF16),
            pltpu.VMEM(fwd.shape, BF16),
            dma((8,)),
            dma((STEPS, 4)),
            dma((STEPS, 4)),
            dma((STEPS, 3)),
            dma((STEPS, 3)),
            dma((STEPS, 3)),
            dma((STEPS, 3)),
        ],
        compiler_params=pltpu.CompilerParams(
            collective_id=0, has_side_effects=True, vmem_limit_bytes=58 * 1024 * 1024
        ),
    )(
        state_in,
        metric,
        base_in,
        jnp.transpose(edge_list, (1, 0, 2)),
        jnp.transpose(flips, (1, 0, 2)),
        jnp.asarray(deriv),
        jnp.asarray(span),
        jnp.asarray(fwd),
    )
    return jnp.transpose(result.reshape(3, NODES, NODES, LOCAL, ELEMS), (0, 3, 1, 2, 4))


def solution(mesh):
    placed = (
        P(None, "plane", None, None, "dom"),
        P(None, "dom"),
        P(None, None, ("dom", "plane")),
        P("dom", None, None),
        P("dom", None, None),
    )
    return jax.shard_map(
        functools.partial(shards, mesh.shape["dom"]),
        mesh=mesh,
        in_specs=placed,
        out_specs=P(None, "plane", None, None, "dom"),
        check_vma=False,
    )
```

```python
import functools

import jax
import jax.numpy as jnp
import ml_dtypes
import numpy as np
from jax import lax
from jax.experimental import pallas as pl
from jax.experimental.pallas import tpu as pltpu
from jax.sharding import PartitionSpec as P

MODES = 64
STEPS = 2
NODES = 9
NPTS = NODES * NODES
ELEMS = 32
PLANE = 16
LOCAL = MODES // PLANE
SPAN_PTS = NPTS * ELEMS // PLANE
CAP = 24
REACH = 2
STEP_SIZE = 0.01
VISCOSITY = 0.02

ROWS = 88
KROWS = 96
WIRE = 48
BACK = 8
REST = SPAN_PTS - 128
FLOWS = 12 * STEPS

F32 = jnp.float32
BF16 = jnp.bfloat16
MESH_ID = pl.DeviceIdType.MESH


def split_table(table):
    hi = table.astype(np.float32).astype(ml_dtypes.bfloat16)
    lo = (table - hi.astype(np.float64)).astype(np.float32).astype(ml_dtypes.bfloat16)
    return np.concatenate([hi, hi, lo], axis=1)


def derivative_tables():
    order = NODES - 1
    ids = np.arange(NODES)
    coords = -np.cos(np.pi * ids / order)
    weight = np.where((ids == 0) | (ids == order), 2.0, 1.0)
    table = np.zeros((NODES, NODES))
    for a in range(NODES):
        for i in range(NODES):
            if a != i:
                table[a, i] = weight[a] / weight[i] * (-1.0) ** (a + i) / (coords[a] - coords[i])
    table -= np.diag(table.sum(axis=1))
    eye = np.eye(NODES)
    along_xi, along_eta = np.kron(table, eye), np.kron(eye, table)
    ops = [
        along_xi,
        along_eta,
        along_xi @ along_xi,
        along_xi @ along_eta,
        along_eta @ along_eta,
    ]
    stacked = np.zeros((len(ops) * ROWS, KROWS))
    for at, op in enumerate(ops):
        stacked[at * ROWS : at * ROWS + NPTS, :NPTS] = op
    return split_table(stacked)


def span_tables():
    modes = np.arange(MODES)
    wave = (modes + 1) // 2
    cosine = (modes % 2 == 1) | (modes == 0)
    angles = 2.0 * np.pi * ((np.arange(MODES)[:, None] * wave[None, :]) % MODES) / MODES
    basis = np.where(cosine[None, :], np.cos(angles), np.sin(angles))
    slope = np.where(cosine[None, :], -wave * np.sin(angles), wave * np.cos(angles))
    scale = np.where((modes == 0) | (modes == MODES - 1), 1.0 / MODES, 2.0 / MODES)
    forward = basis.T * scale[:, None]
    order = (np.arange(PLANE)[None, :] * LOCAL + np.arange(LOCAL)[:, None]).reshape(-1)
    span = np.concatenate([basis[:, order], slope[:, order]], axis=0)
    return split_table(span), split_table(forward[order])


def halves(x):
    hi = x.astype(BF16)
    return hi, (x - hi.astype(F32)).astype(BF16)


def three(x):
    hi, lo = halves(x)
    return jnp.concatenate([hi, lo, hi], axis=0)


def dot(a, b):
    return jnp.dot(a, b, preferred_element_type=F32)


def swap_blocks(parts):
    shape = parts[0].shape
    lane = lax.broadcasted_iota(jnp.int32, shape, 1)
    even = (lane // 32) % 2 == 0
    low = lane < 64
    a0, a1, a2, a3 = parts

    def near(x, y):
        return (
            jnp.where(even, x, pltpu.roll(y, 32, 1)),
            jnp.where(even, pltpu.roll(x, 96, 1), y),
        )

    def far(x, y):
        moved = pltpu.roll(jnp.where(low, y, x), 64, 1)
        return jnp.where(low, x, moved), jnp.where(low, moved, y)

    b0, b1 = near(a0, a1)
    b2, b3 = near(a2, a3)
    c0, c2 = far(b0, b2)
    c1, c3 = far(b1, b3)
    return [c0, c1, c2, c3]


def turn(x, shift):
    return pltpu.roll(x, shift % 128, 1) if shift % 128 else x


STATE_AT = ((0, 8, 16), (0, 16, 32))
GRAD_AT = ((24, 32, 40), (8, 24, 40))
CHUNKS = (((0, 24), (24, 8), (32, 8), (40, 8)), ((0, 16), (16, 16), (32, 8), (40, 8)))
DISTANCES = (8, 9, 7, 6, 10, 11, 5, 4, 12, 13, 3, 2, 14, 15, 1)


def kernel(
    n_dom,
    adj_ref,
    met_ref,
    base_ref,
    edge_ref,
    flip_ref,
    deriv_ref,
    span_ref,
    fwd_ref,
    out_ref,
    state,
    grads,
    base_in,
    base_rows,
    base_head,
    base_tail,
    send_out,
    recv_out,
    send_back,
    recv_back,
    edge_out,
    edge_in,
    trace_a,
    trace_b,
    sums,
    send_hot,
    recv_hot,
    inv_weight,
    metrics,
    slot_ids,
    adj_in,
    met_in,
    deriv_in,
    edge_ids,
    flip_ids,
    span_in,
    fwd_in,
    load_sem,
    store_sem,
    out_send,
    out_recv,
    back_send,
    back_recv,
    edge_send,
    edge_recv,
):
    dom = lax.axis_index("dom")
    me = lax.axis_index("plane")

    barrier = pltpu.get_barrier_semaphore()

    others = [0, 4, 1, 3]
    for distance in DISTANCES:
        pl.semaphore_signal(
            barrier, inc=1, device_id=(dom, lax.rem(me + distance, PLANE)), device_id_type=MESH_ID
        )
    for block in others:
        pl.semaphore_signal(
            barrier,
            inc=1,
            device_id=(lax.rem(dom + block - REACH + n_dom, n_dom), me),
            device_id_type=MESH_ID,
        )

    loads = {}
    for at, (name, source, target) in enumerate(
        (
            ("state", adj_ref, adj_in),
            ("metric", met_ref, met_in),
            ("deriv", deriv_ref, deriv_in),
            ("base", base_ref, base_in),
            ("edges", edge_ref, edge_ids),
            ("flips", flip_ref, flip_ids),
            ("span", span_ref, span_in),
            ("forward", fwd_ref, fwd_in),
        )
    ):
        loads[name] = pltpu.make_async_copy(source, target, load_sem.at[at])
        loads[name].start()

    def out_copy(step, chunk, distance):
        peer = lax.rem(me + distance, PLANE)
        start, rows = CHUNKS[step][chunk]
        return pltpu.make_async_remote_copy(
            src_ref=send_out.at[step, pl.ds(pl.multiple_of(peer * WIRE + start, 8), rows)],
            dst_ref=recv_out.at[step, pl.ds(pl.multiple_of(me * WIRE + start, 8), rows)],
            send_sem=out_send.at[step, chunk],
            recv_sem=out_recv.at[step, chunk],
            device_id=(dom, peer),
            device_id_type=MESH_ID,
        )

    def back_copy(step, comp, distance):
        peer = lax.rem(me + distance, PLANE)
        return pltpu.make_async_remote_copy(
            src_ref=send_back.at[step, comp, pl.ds(pl.multiple_of(peer * BACK, 8), BACK)],
            dst_ref=recv_back.at[step, comp, pl.ds(pl.multiple_of(me * BACK, 8), BACK)],
            send_sem=back_send.at[step, comp],
            recv_sem=back_recv.at[step, comp],
            device_id=(dom, peer),
            device_id_type=MESH_ID,
        )

    def edge_copy(step, comp, block):
        return pltpu.make_async_remote_copy(
            src_ref=edge_out.at[step, comp, pl.ds(block * CAP, CAP)],
            dst_ref=edge_in.at[step, comp, pl.ds((2 * REACH - block) * CAP, CAP)],
            send_sem=edge_send.at[step, comp],
            recv_sem=edge_recv.at[step, comp],
            device_id=(lax.rem(dom + block - REACH + n_dom, n_dom), me),
            device_id_type=MESH_ID,
        )

    def all_of(source, target, rows, send_sem, recv_sem):
        return pltpu.make_async_remote_copy(
            src_ref=source.at[pl.ds(0, rows)],
            dst_ref=target.at[pl.ds(0, rows)],
            send_sem=send_sem,
            recv_sem=recv_sem,
            device_id=(dom, lax.rem(me + 1, PLANE)),
            device_id_type=MESH_ID,
        )

    def all_out(step, chunk):
        rows = (PLANE - 1) * CHUNKS[step][chunk][1]
        sems = out_send.at[step, chunk], out_recv.at[step, chunk]
        return all_of(send_out.at[step], recv_out.at[step], rows, *sems)

    def all_back(step, comp):
        rows = (PLANE - 1) * BACK
        sems = back_send.at[step, comp], back_recv.at[step, comp]
        return all_of(send_back.at[step, comp], recv_back.at[step, comp], rows, *sems)

    def all_edges(step, comp):
        sems = edge_send.at[step, comp], edge_recv.at[step, comp]
        return all_of(edge_out.at[step, comp], edge_in.at[step, comp], 2 * REACH * CAP, *sems)

    def each_peer(what):
        for distance in DISTANCES:
            what(distance)

    loads["state"].wait()
    for comp in range(3):
        for mode in range(LOCAL):
            state[comp, 0:NPTS, ELEMS * mode : ELEMS * (mode + 1)] = adj_in[comp, :, mode, :]
        state[comp, NPTS:KROWS, :] = jnp.zeros((KROWS - NPTS, 128), F32)
    loads["metric"].wait()
    for row in range(4):
        for group in range(4):
            metrics[row : row + 1, ELEMS * group : ELEMS * (group + 1)] = met_in[row : row + 1, :]
    xi_x, xi_y = metrics[0:1, :], metrics[1:2, :]
    eta_x, eta_y = metrics[2:3, :], metrics[3:4, :]

    lane_row = lax.broadcasted_iota(jnp.int32, (1, 128), 1)
    owner_lane = lax.broadcasted_iota(jnp.int32, (PLANE, 128), 1)
    owner_start = 2 * lax.broadcasted_iota(jnp.int32, (PLANE, 128), 0)
    after = owner_lane >= owner_start
    places = []
    for comp in range(3):
        place = (owner_lane - owner_start + (128 - REST * comp)) % 128
        places.append(place < REST)
    wave = ((LOCAL * me + lane_row // ELEMS + 1) // 2).astype(F32)

    def split_state(comp):
        return three(state[comp])

    def derive(step, comp, rhs):
        first = dot(deriv_in[0 : 2 * ROWS, :], rhs)
        along_xi, along_eta = first[0:ROWS, :], first[ROWS : 2 * ROWS, :]
        grads[2 * comp, 0:ROWS, :] = xi_x * along_xi + eta_x * along_eta
        grads[2 * comp + 1, 0:ROWS, :] = xi_y * along_xi + eta_y * along_eta

        def nodes(field, k):
            rows = pl.ds(k, PLANE, stride=5)
            return grads[2 * comp + field - 1, rows, :] if field else state[comp, rows, :]

        zeros = jnp.zeros((PLANE, 128), F32)

        def put(at, mode, rows):
            send_out[step, pl.ds(at + mode, PLANE, stride=WIRE), :] = rows

        early = swap_blocks([nodes(0, 4), nodes(0, 5), nodes(1, 4), nodes(1, 5)])
        late = swap_blocks([nodes(2, 4), nodes(2, 5), zeros, zeros])
        packed = [zeros] * LOCAL
        to = (STATE_AT[step][comp], GRAD_AT[step][comp], GRAD_AT[step][comp] + LOCAL)
        for field in range(3):
            heads = swap_blocks([nodes(field, k) for k in range(4)])
            both, side = (late, 0) if field == 2 else (early, 64 * field)
            for mode in range(LOCAL):
                put(to[field], mode, jnp.where(after, heads[mode], turn(both[mode], -side)))
                packed[mode] = jnp.where(
                    places[field], turn(both[mode], REST * field - side), packed[mode]
                )
        for mode in range(LOCAL):
            put(STATE_AT[step][comp] + LOCAL, mode, packed[mode])

    def send_chunk(step, chunk):
        each_peer(lambda distance: out_copy(step, chunk, distance).start())

    def keep_chunk(step, chunk):
        start, rows = CHUNKS[step][chunk]
        mine = pl.ds(pl.multiple_of(me * WIRE + start, 8), rows)
        recv_out[step, mine, :] = send_out[step, mine, :]

    def diffuse(comp, rhs):
        second = dot(deriv_in[2 * ROWS : 5 * ROWS, :], rhs)
        factor = STEP_SIZE * VISCOSITY
        keep = 1.0 - factor * (wave * wave)
        both_xi = factor * (xi_x * xi_x + xi_y * xi_y)
        mixed = (2.0 * factor) * (xi_x * eta_x + xi_y * eta_y)
        both_eta = factor * (eta_x * eta_x + eta_y * eta_y)
        state[comp, 0:ROWS, :] = keep * state[comp, 0:ROWS, :] + (
            both_xi * second[0:ROWS, :]
            + mixed * second[ROWS : 2 * ROWS, :]
            + both_eta * second[2 * ROWS : 3 * ROWS, :]
        )

    def gather_base():
        loads["base"].wait()

        def gather(block, carry):
            lanes = pl.ds(pl.multiple_of(128 * block, 128), 128)
            rows = pl.ds(pl.multiple_of(FLOWS * block, 8), FLOWS)
            base_rows[rows, :] = base_in[:, :, lanes].reshape(FLOWS, 128)
            return carry

        lax.fori_loop(0, NPTS, gather, 0)
        base_rows[FLOWS * NPTS :, :] = jnp.zeros((2 * FLOWS, 128), F32)

    def arrange_base():
        lane = lax.broadcasted_iota(jnp.int32, (FLOWS, 128), 1)
        point = (lane - 2 * me + 128) % 128

        def body(n, carry):
            start = SPAN_PTS * n
            block = start // 128
            shift = start - 128 * block
            back = lax.rem(128 - shift + 2 * me, 128)
            early = point < 128 - shift
            rolled = []
            for at in range(3):
                rows = pl.ds(pl.multiple_of(FLOWS * (block + at), 8), FLOWS)
                rolled.append(pltpu.roll(base_rows[rows, :], back, 1))
            to = pl.ds(n, FLOWS, stride=MODES)
            base_head[to, :] = jnp.where(early, rolled[0], rolled[1])
            base_tail[to, :] = jnp.where(
                point < REST, jnp.where(early, rolled[1], rolled[2]), 0.0
            )
            return carry

        lax.fori_loop(0, MODES, body, 0)

    def prepare_edges():
        loads["edges"].wait()
        loads["flips"].wait()
        slot_ids[...] = jnp.full((16, 128), -1, jnp.int32)
        for block in range(2 * REACH + 1):
            lanes = slice(CAP * block, CAP * (block + 1))
            slot_ids[0:1, lanes] = edge_ids[block]
            slot_ids[8:9, lanes] = flip_ids[block]
        own, flip = slot_ids[0:1, :], slot_ids[8:9, :]
        odd = lane_row % 2 == 1
        paired = jnp.where(odd, pltpu.roll(own, 1, 1), pltpu.roll(own, 127, 1))
        inner = (lane_row >= CAP * REACH) & (lane_row < CAP * (REACH + 1))
        given = jnp.where(inner, paired, own)
        edge_row = lax.broadcasted_iota(jnp.int32, (128, 128), 0)
        hot = jnp.where(edge_row == own, 1.0, 0.0).astype(F32)
        recv_hot[:, 0:128] = hot.astype(BF16)
        recv_hot[:, 128:256] = hot.astype(BF16)
        gave = jnp.where(edge_row == given, 1.0, 0.0).astype(F32)
        turned = jnp.where(flip == 1, gave, 0.0)
        straight = (gave - turned).T.astype(BF16)
        turned = turned.T.astype(BF16)
        for part in range(2):
            send_hot[:, 256 * part : 256 * part + 128] = straight
            send_hot[:, 256 * part + 128 : 256 * part + 256] = turned
        counts = jnp.sum(hot.T, axis=0, keepdims=True)
        spread = []
        for edge in range(4):
            one = jnp.where(lane_row // ELEMS == edge, counts, 0.0)
            one = one + pltpu.roll(one, 64, 1)
            spread.append(one + pltpu.roll(one, 32, 1))
        inv_weight[...] = jnp.ones((KROWS, 128), F32)
        for edge, rows in enumerate(edge_rows):
            inv_weight[rows, :] = inv_weight[rows, :] + spread[edge]
        inv_weight[...] = 1.0 / inv_weight[...]
        trace_b[...] = jnp.zeros((40, 256), F32)
        edge_out[...] = jnp.zeros((STEPS, 3, 128, 128), F32)
        edge_in[:, :, 120:128, :] = jnp.zeros((STEPS, 3, 8, 128), F32)

    def physical(step):
        def column(at):
            return jnp.concatenate(
                [
                    recv_out[step, pl.ds(at + mode, PLANE, stride=WIRE), :]
                    for mode in range(LOCAL)
                ],
                axis=0,
            )

        for chunk in range(1 if step == 0 else 3):
            all_out(step, chunk).wait_recv()
        columns = []
        for comp in range(3):
            columns += [column(STATE_AT[step][comp]), column(STATE_AT[step][comp] + LOCAL)]
        of_state = dot(span_in[...], three(jnp.concatenate(columns, axis=1)))

        def flow(base, index):
            row = MODES * (STEPS * index + step)
            return base[row : row + MODES, :]

        def product(comp, base, side, along_x, along_y):
            def now(i, slope=False):
                lanes = 128 * (2 * i + side)
                rows = slice(MODES, 2 * MODES) if slope else slice(0, MODES)
                return of_state[rows, lanes : lanes + 128]

            term = (
                flow(base, 0) * along_x + flow(base, 1) * along_y + flow(base, 2) * now(comp, True)
            )
            return term - (
                now(0) * flow(base, 3 + comp)
                + now(1) * flow(base, 6 + comp)
                + now(2) * flow(base, 9 + comp)
            )

        for comp in range(3):
            if step == 0 or comp == 2:
                all_out(step, comp + 1).wait_recv()
            at = GRAD_AT[step][comp]
            rhs = three(jnp.concatenate([column(at), column(at + LOCAL)], axis=1))
            of_grads = dot(span_in[0:MODES, :], rhs)
            first = product(comp, base_head, 0, of_grads[:, 0:128], of_grads[:, 128:256])
            rest_now = of_state[0:MODES, 128 * (2 * comp + 1) : 128 * (2 * comp + 2)]
            rest = product(comp, base_tail, 1, turn(rest_now, -REST), turn(rest_now, -2 * REST))
            back = dot(fwd_in[...], three(jnp.concatenate([first, rest], axis=1)))
            for at in range(2):
                for mode in range(LOCAL):
                    send_back[step, comp, pl.ds(at * LOCAL + mode, PLANE, stride=BACK), :] = back[
                        PLANE * mode : PLANE * (mode + 1), 128 * at : 128 * at + 128
                    ]
            each_peer(lambda distance, comp=comp: back_copy(step, comp, distance).start())
            mine = pl.ds(pl.multiple_of(me * BACK, 8), BACK)
            recv_back[step, comp, mine, :] = send_back[step, comp, mine, :]

    first_col, last_col = pl.ds(0, NODES, stride=NODES), pl.ds(8, NODES, stride=NODES)
    edge_rows = (first_col, slice(72, 81), last_col, slice(0, 9))

    def update(step, comp):
        all_back(step, comp).wait_recv()

        def came(at):
            return recv_back[step, comp, pl.ds(at, PLANE, stride=BACK), :]

        firsts, lasts = [], []
        for mode in range(LOCAL):
            moved = came(mode)
            last = jnp.where(places[0], came(LOCAL + mode), 0.0)
            firsts.append(jnp.where(after, moved, 0.0))
            lasts.append(jnp.where(after, last, moved))
        for k, rate in enumerate(swap_blocks(firsts) + swap_blocks(lasts)[:2]):
            rows = pl.ds(k, PLANE, stride=5)
            state[comp, rows, :] = state[comp, rows, :] + STEP_SIZE * rate

    def give_edges(step, comp):
        traces = swap_blocks([state[comp, rows, :] for rows in edge_rows])
        for mode in range(LOCAL):
            trace_a[mode * 16 : mode * 16 + NODES, :] = traces[mode]
        for i in range(NODES):
            rows = trace_a[pl.ds(i, LOCAL, stride=16), :]
            trace_b[LOCAL * i : LOCAL * (i + 1), 0:128] = rows
            trace_b[LOCAL * (8 - i) : LOCAL * (9 - i), 128:256] = rows
        hi, lo = halves(trace_b[...])
        given = lax.dot_general(
            send_hot[...],
            jnp.concatenate([hi, lo], axis=1),
            (((1,), (1,)), ((), ())),
            preferred_element_type=F32,
        )
        edge_out[step, comp, :, 0:40] = given
        for block in others:
            edge_copy(step, comp, block).start()
        inner = slice(CAP * REACH, CAP * (REACH + 1))
        edge_in[step, comp, inner, :] = edge_out[step, comp, inner, :]

    def take_edges(step, comp):
        all_edges(step, comp).wait_recv()
        hi, lo = halves(edge_in[step, comp])
        sums[...] = dot(recv_hot[...], jnp.concatenate([hi, lo], axis=0)).T
        parts = swap_blocks([sums[pl.ds(mode, NODES, stride=LOCAL), :] for mode in range(LOCAL)])
        for rows, part in zip(edge_rows, parts):
            state[comp, rows, :] = state[comp, rows, :] + part
        state[comp, 0:ROWS, :] = state[comp, 0:ROWS, :] * inv_weight[0:ROWS, :]

    loads["deriv"].wait()
    halved = [split_state(comp) for comp in range(3)]
    for comp in range(3):
        derive(0, comp, halved[comp])
    prepare_edges()
    gather_base()
    pl.semaphore_wait(barrier, PLANE - 1 + len(others))
    for chunk in range(4):
        send_chunk(0, chunk)
    for chunk in range(4):
        keep_chunk(0, chunk)
    for comp in range(3):
        diffuse(comp, halved[comp])
    arrange_base()
    loads["span"].wait()
    loads["forward"].wait()
    physical(0)
    for comp in range(3):
        update(0, comp)
        give_edges(0, comp)
    halved = []
    for comp in range(3):
        take_edges(0, comp)
        halved.append(split_state(comp))
        derive(1, comp, halved[comp])
        for chunk in (comp,) if comp < 2 else (2, 3):
            send_chunk(1, chunk)
    for chunk in range(4):
        keep_chunk(1, chunk)
    for comp in range(3):
        diffuse(comp, halved[comp])
    physical(1)
    for comp in range(3):
        update(1, comp)
        give_edges(1, comp)
    for step in range(STEPS):
        for chunk in range(4):
            all_out(step, chunk).wait_send()
        for comp in range(3):
            all_back(step, comp).wait_send()
            all_edges(step, comp).wait_send()
    stores = []
    for comp in range(3):
        take_edges(1, comp)
        store = pltpu.make_async_copy(
            state.at[comp, pl.ds(0, NPTS)], out_ref.at[comp], store_sem.at[comp]
        )
        store.start()
        stores.append(store)
    for store in stores:
        store.wait()


def shards(n_dom, adjoint, metric, base_flow, edge_list, flips):
    state_in = jnp.transpose(adjoint, (0, 2, 3, 1, 4)).reshape(3, NPTS, LOCAL, ELEMS)
    base_in = jnp.transpose(base_flow, (1, 0, 2))
    deriv = derivative_tables()
    span, fwd = span_tables()
    dma = pltpu.SemaphoreType.DMA
    result = pl.pallas_call(
        functools.partial(kernel, n_dom),
        out_shape=jax.ShapeDtypeStruct((3, NPTS, 128), F32),
        in_specs=[pl.BlockSpec(memory_space=pltpu.HBM)] * 8,
        out_specs=pl.BlockSpec(memory_space=pltpu.HBM),
        scratch_shapes=[
            pltpu.VMEM((3, KROWS, 128), F32),
            pltpu.VMEM((6, KROWS, 128), F32),
            pltpu.VMEM((12, STEPS, 128 * NPTS), F32),
            pltpu.VMEM((FLOWS * (NPTS + 2), 128), F32),
            pltpu.VMEM((FLOWS * MODES, 128), F32),
            pltpu.VMEM((FLOWS * MODES, 128), F32),
            pltpu.VMEM((STEPS, PLANE * WIRE, 128), F32),
            pltpu.VMEM((STEPS, PLANE * WIRE, 128), F32),
            pltpu.VMEM((STEPS, 3, PLANE * BACK, 128), F32),
            pltpu.VMEM((STEPS, 3, PLANE * BACK, 128), F32),
            pltpu.VMEM((STEPS, 3, 128, 128), F32),
            pltpu.VMEM((STEPS, 3, 128, 128), F32),
            pltpu.VMEM((LOCAL * 16, 128), F32),
            pltpu.VMEM((40, 256), F32),
            pltpu.VMEM((128, 128), F32),
            pltpu.VMEM((128, 512), BF16),
            pltpu.VMEM((128, 256), BF16),
            pltpu.VMEM((KROWS, 128), F32),
            pltpu.VMEM((8, 128), F32),
            pltpu.VMEM((16, 128), jnp.int32),
            pltpu.VMEM((3, NPTS, LOCAL, ELEMS), F32),
            pltpu.VMEM((4, ELEMS), F32),
            pltpu.VMEM(deriv.shape, BF16),
            pltpu.VMEM((2 * REACH + 1, 1, CAP), jnp.int32),
            pltpu.VMEM((2 * REACH + 1, 1, CAP), jnp.int32),
            pltpu.VMEM(span.shape, BF16),
            pltpu.VMEM(fwd.shape, BF16),
            dma((8,)),
            dma((3,)),
            dma((STEPS, 4)),
            dma((STEPS, 4)),
            dma((STEPS, 3)),
            dma((STEPS, 3)),
            dma((STEPS, 3)),
            dma((STEPS, 3)),
        ],
        compiler_params=pltpu.CompilerParams(
            collective_id=0, has_side_effects=True, vmem_limit_bytes=58 * 1024 * 1024
        ),
    )(
        state_in,
        metric,
        base_in,
        jnp.transpose(edge_list, (1, 0, 2)),
        jnp.transpose(flips, (1, 0, 2)),
        jnp.asarray(deriv),
        jnp.asarray(span),
        jnp.asarray(fwd),
    )
    return jnp.transpose(result.reshape(3, NODES, NODES, LOCAL, ELEMS), (0, 3, 1, 2, 4))


def solution(mesh):
    placed = (
        P(None, "plane", None, None, "dom"),
        P(None, "dom"),
        P(None, None, ("dom", "plane")),
        P("dom", None, None),
        P("dom", None, None),
    )
    return jax.shard_map(
        functools.partial(shards, mesh.shape["dom"]),
        mesh=mesh,
        in_specs=placed,
        out_specs=P(None, "plane", None, None, "dom"),
        check_vma=False,
    )
```

```python
import functools

import jax
import jax.numpy as jnp
import ml_dtypes
import numpy as np
from jax import lax
from jax.experimental import pallas as pl
from jax.experimental.pallas import tpu as pltpu
from jax.sharding import PartitionSpec as P

MODES = 64
STEPS = 2
NODES = 9
NPTS = NODES * NODES
ELEMS = 32
PLANE = 16
LOCAL = MODES // PLANE
SPAN_PTS = NPTS * ELEMS // PLANE
CAP = 24
REACH = 2
STEP_SIZE = 0.01
VISCOSITY = 0.02

ROWS = 88
KROWS = 96
WIRE = 48
BACK = 8
REST = SPAN_PTS - 128
FLOWS = 12 * STEPS

F32 = jnp.float32
BF16 = jnp.bfloat16
MESH_ID = pl.DeviceIdType.MESH


def split_table(table):
    hi = table.astype(np.float32).astype(ml_dtypes.bfloat16)
    lo = (table - hi.astype(np.float64)).astype(np.float32).astype(ml_dtypes.bfloat16)
    return np.concatenate([hi, hi, lo], axis=1)


def derivative_tables():
    order = NODES - 1
    ids = np.arange(NODES)
    coords = -np.cos(np.pi * ids / order)
    weight = np.where((ids == 0) | (ids == order), 2.0, 1.0)
    table = np.zeros((NODES, NODES))
    for a in range(NODES):
        for i in range(NODES):
            if a != i:
                table[a, i] = weight[a] / weight[i] * (-1.0) ** (a + i) / (coords[a] - coords[i])
    table -= np.diag(table.sum(axis=1))
    eye = np.eye(NODES)
    along_xi, along_eta = np.kron(table, eye), np.kron(eye, table)
    ops = [
        along_xi,
        along_eta,
        along_xi @ along_xi,
        along_xi @ along_eta,
        along_eta @ along_eta,
    ]
    stacked = np.zeros((len(ops) * ROWS, KROWS))
    for at, op in enumerate(ops):
        stacked[at * ROWS : at * ROWS + NPTS, :NPTS] = op
    return split_table(stacked)


def span_tables():
    modes = np.arange(MODES)
    wave = (modes + 1) // 2
    cosine = (modes % 2 == 1) | (modes == 0)
    angles = 2.0 * np.pi * ((np.arange(MODES)[:, None] * wave[None, :]) % MODES) / MODES
    basis = np.where(cosine[None, :], np.cos(angles), np.sin(angles))
    slope = np.where(cosine[None, :], -wave * np.sin(angles), wave * np.cos(angles))
    scale = np.where((modes == 0) | (modes == MODES - 1), 1.0 / MODES, 2.0 / MODES)
    forward = basis.T * scale[:, None]
    order = (np.arange(PLANE)[None, :] * LOCAL + np.arange(LOCAL)[:, None]).reshape(-1)
    span = np.concatenate([basis[:, order], slope[:, order]], axis=0)
    return split_table(span), split_table(forward[order])


def halves(x):
    hi = x.astype(BF16)
    return hi, (x - hi.astype(F32)).astype(BF16)


def three(x):
    hi, lo = halves(x)
    return jnp.concatenate([hi, lo, hi], axis=0)


def dot(a, b):
    return jnp.dot(a, b, preferred_element_type=F32)


def swap_blocks(parts):
    shape = parts[0].shape
    lane = lax.broadcasted_iota(jnp.int32, shape, 1)
    even = (lane // 32) % 2 == 0
    low = lane < 64
    a0, a1, a2, a3 = parts

    def near(x, y):
        return (
            jnp.where(even, x, pltpu.roll(y, 32, 1)),
            jnp.where(even, pltpu.roll(x, 96, 1), y),
        )

    def far(x, y):
        moved = pltpu.roll(jnp.where(low, y, x), 64, 1)
        return jnp.where(low, x, moved), jnp.where(low, moved, y)

    b0, b1 = near(a0, a1)
    b2, b3 = near(a2, a3)
    c0, c2 = far(b0, b2)
    c1, c3 = far(b1, b3)
    return [c0, c1, c2, c3]


def turn(x, shift):
    return pltpu.roll(x, shift % 128, 1) if shift % 128 else x


STATE_AT = ((0, 8, 16), (0, 16, 32))
GRAD_AT = ((24, 32, 40), (8, 24, 40))
CHUNKS = (((0, 24), (24, 8), (32, 8), (40, 8)), ((0, 16), (16, 16), (32, 8), (40, 8)))
DISTANCES = (8, 9, 7, 6, 10, 11, 5, 4, 12, 13, 3, 2, 14, 15, 1)


def kernel(
    n_dom,
    adj_ref,
    met_ref,
    base_ref,
    edge_ref,
    flip_ref,
    deriv_ref,
    span_ref,
    fwd_ref,
    out_ref,
    state,
    grads,
    base_in,
    base_rows,
    base_head,
    base_tail,
    send_out,
    recv_out,
    send_back,
    recv_back,
    edge_out,
    edge_in,
    trace_a,
    trace_b,
    sums,
    send_hot,
    recv_hot,
    inv_weight,
    metrics,
    slot_ids,
    adj_in,
    met_in,
    deriv_in,
    edge_ids,
    flip_ids,
    span_in,
    fwd_in,
    load_sem,
    store_sem,
    out_send,
    out_recv,
    back_send,
    back_recv,
    edge_send,
    edge_recv,
):
    dom = lax.axis_index("dom")
    me = lax.axis_index("plane")

    barrier = pltpu.get_barrier_semaphore()

    others = [0, 4, 1, 3]
    for distance in DISTANCES:
        pl.semaphore_signal(
            barrier, inc=1, device_id=(dom, lax.rem(me + distance, PLANE)), device_id_type=MESH_ID
        )
    for block in others:
        pl.semaphore_signal(
            barrier,
            inc=1,
            device_id=(lax.rem(dom + block - REACH + n_dom, n_dom), me),
            device_id_type=MESH_ID,
        )

    loads = {}
    for at, (name, source, target) in enumerate(
        (
            ("state", adj_ref, adj_in),
            ("metric", met_ref, met_in),
            ("deriv", deriv_ref, deriv_in),
            ("base", base_ref, base_in),
            ("edges", edge_ref, edge_ids),
            ("flips", flip_ref, flip_ids),
            ("span", span_ref, span_in),
            ("forward", fwd_ref, fwd_in),
        )
    ):
        loads[name] = pltpu.make_async_copy(source, target, load_sem.at[at])
        loads[name].start()

    def out_copy(step, chunk, distance):
        peer = lax.rem(me + distance, PLANE)
        start, rows = CHUNKS[step][chunk]
        return pltpu.make_async_remote_copy(
            src_ref=send_out.at[step, pl.ds(pl.multiple_of(peer * WIRE + start, 8), rows)],
            dst_ref=recv_out.at[step, pl.ds(pl.multiple_of(me * WIRE + start, 8), rows)],
            send_sem=out_send.at[step, chunk],
            recv_sem=out_recv.at[step, chunk],
            device_id=(dom, peer),
            device_id_type=MESH_ID,
        )

    def back_copy(step, comp, distance):
        peer = lax.rem(me + distance, PLANE)
        return pltpu.make_async_remote_copy(
            src_ref=send_back.at[step, comp, pl.ds(pl.multiple_of(peer * BACK, 8), BACK)],
            dst_ref=recv_back.at[step, comp, pl.ds(pl.multiple_of(me * BACK, 8), BACK)],
            send_sem=back_send.at[step, comp],
            recv_sem=back_recv.at[step, comp],
            device_id=(dom, peer),
            device_id_type=MESH_ID,
        )

    def edge_copy(step, comp, block):
        return pltpu.make_async_remote_copy(
            src_ref=edge_out.at[step, comp, pl.ds(block * CAP, CAP)],
            dst_ref=edge_in.at[step, comp, pl.ds((2 * REACH - block) * CAP, CAP)],
            send_sem=edge_send.at[step, comp],
            recv_sem=edge_recv.at[step, comp],
            device_id=(lax.rem(dom + block - REACH + n_dom, n_dom), me),
            device_id_type=MESH_ID,
        )

    def all_of(source, target, rows, send_sem, recv_sem):
        return pltpu.make_async_remote_copy(
            src_ref=source.at[pl.ds(0, rows)],
            dst_ref=target.at[pl.ds(0, rows)],
            send_sem=send_sem,
            recv_sem=recv_sem,
            device_id=(dom, lax.rem(me + 1, PLANE)),
            device_id_type=MESH_ID,
        )

    def all_out(step, chunk):
        rows = (PLANE - 1) * CHUNKS[step][chunk][1]
        sems = out_send.at[step, chunk], out_recv.at[step, chunk]
        return all_of(send_out.at[step], recv_out.at[step], rows, *sems)

    def all_back(step, comp):
        rows = (PLANE - 1) * BACK
        sems = back_send.at[step, comp], back_recv.at[step, comp]
        return all_of(send_back.at[step, comp], recv_back.at[step, comp], rows, *sems)

    def all_edges(step, comp):
        sems = edge_send.at[step, comp], edge_recv.at[step, comp]
        return all_of(edge_out.at[step, comp], edge_in.at[step, comp], 2 * REACH * CAP, *sems)

    def each_peer(what):
        for distance in DISTANCES:
            what(distance)

    loads["state"].wait()
    for comp in range(3):
        for mode in range(LOCAL):
            state[comp, 0:NPTS, ELEMS * mode : ELEMS * (mode + 1)] = adj_in[comp, :, mode, :]
        state[comp, NPTS:KROWS, :] = jnp.zeros((KROWS - NPTS, 128), F32)
    loads["metric"].wait()
    for row in range(4):
        for group in range(4):
            metrics[row : row + 1, ELEMS * group : ELEMS * (group + 1)] = met_in[row : row + 1, :]
    xi_x, xi_y = metrics[0:1, :], metrics[1:2, :]
    eta_x, eta_y = metrics[2:3, :], metrics[3:4, :]

    lane_row = lax.broadcasted_iota(jnp.int32, (1, 128), 1)
    owner_lane = lax.broadcasted_iota(jnp.int32, (PLANE, 128), 1)
    owner_start = 2 * lax.broadcasted_iota(jnp.int32, (PLANE, 128), 0)
    after = owner_lane >= owner_start
    places = []
    for comp in range(3):
        place = (owner_lane - owner_start + (128 - REST * comp)) % 128
        places.append(place < REST)
    wave = ((LOCAL * me + lane_row // ELEMS + 1) // 2).astype(F32)

    def split_state(comp):
        return three(state[comp])

    def derive(step, comp, rhs):
        first = dot(deriv_in[0 : 2 * ROWS, :], rhs)
        along_xi, along_eta = first[0:ROWS, :], first[ROWS : 2 * ROWS, :]
        grads[2 * comp, 0:ROWS, :] = xi_x * along_xi + eta_x * along_eta
        grads[2 * comp + 1, 0:ROWS, :] = xi_y * along_xi + eta_y * along_eta

        def nodes(field, k):
            rows = pl.ds(k, PLANE, stride=5)
            return grads[2 * comp + field - 1, rows, :] if field else state[comp, rows, :]

        zeros = jnp.zeros((PLANE, 128), F32)

        def put(at, mode, rows):
            send_out[step, pl.ds(at + mode, PLANE, stride=WIRE), :] = rows

        early = swap_blocks([nodes(0, 4), nodes(0, 5), nodes(1, 4), nodes(1, 5)])
        late = swap_blocks([nodes(2, 4), nodes(2, 5), zeros, zeros])
        packed = [zeros] * LOCAL
        to = (STATE_AT[step][comp], GRAD_AT[step][comp], GRAD_AT[step][comp] + LOCAL)
        for field in range(3):
            heads = swap_blocks([nodes(field, k) for k in range(4)])
            both, side = (late, 0) if field == 2 else (early, 64 * field)
            for mode in range(LOCAL):
                put(to[field], mode, jnp.where(after, heads[mode], turn(both[mode], -side)))
                packed[mode] = jnp.where(
                    places[field], turn(both[mode], REST * field - side), packed[mode]
                )
        for mode in range(LOCAL):
            put(STATE_AT[step][comp] + LOCAL, mode, packed[mode])

    def send_chunk(step, chunk):
        each_peer(lambda distance: out_copy(step, chunk, distance).start())

    def keep_chunk(step, chunk):
        start, rows = CHUNKS[step][chunk]
        mine = pl.ds(pl.multiple_of(me * WIRE + start, 8), rows)
        recv_out[step, mine, :] = send_out[step, mine, :]

    def diffuse(comp, rhs):
        second = dot(deriv_in[2 * ROWS : 5 * ROWS, :], rhs)
        factor = STEP_SIZE * VISCOSITY
        keep = 1.0 - factor * (wave * wave)
        both_xi = factor * (xi_x * xi_x + xi_y * xi_y)
        mixed = (2.0 * factor) * (xi_x * eta_x + xi_y * eta_y)
        both_eta = factor * (eta_x * eta_x + eta_y * eta_y)
        state[comp, 0:ROWS, :] = keep * state[comp, 0:ROWS, :] + (
            both_xi * second[0:ROWS, :]
            + mixed * second[ROWS : 2 * ROWS, :]
            + both_eta * second[2 * ROWS : 3 * ROWS, :]
        )

    def gather_base():
        loads["base"].wait()

        def gather(block, carry):
            lanes = pl.ds(pl.multiple_of(128 * block, 128), 128)
            rows = pl.ds(pl.multiple_of(FLOWS * block, 8), FLOWS)
            base_rows[rows, :] = base_in[:, :, lanes].reshape(FLOWS, 128)
            return carry

        lax.fori_loop(0, NPTS, gather, 0)
        base_rows[FLOWS * NPTS :, :] = jnp.zeros((2 * FLOWS, 128), F32)

    def arrange_base():
        lane = lax.broadcasted_iota(jnp.int32, (FLOWS, 128), 1)
        point = (lane - 2 * me + 128) % 128

        def body(n, carry):
            start = SPAN_PTS * n
            block = start // 128
            shift = start - 128 * block
            back = lax.rem(128 - shift + 2 * me, 128)
            early = point < 128 - shift
            rolled = []
            for at in range(3):
                rows = pl.ds(pl.multiple_of(FLOWS * (block + at), 8), FLOWS)
                rolled.append(pltpu.roll(base_rows[rows, :], back, 1))
            to = pl.ds(n, FLOWS, stride=MODES)
            base_head[to, :] = jnp.where(early, rolled[0], rolled[1])
            base_tail[to, :] = jnp.where(
                point < REST, jnp.where(early, rolled[1], rolled[2]), 0.0
            )
            return carry

        lax.fori_loop(0, MODES, body, 0)

    def prepare_edges():
        loads["edges"].wait()
        loads["flips"].wait()
        slot_ids[...] = jnp.full((16, 128), -1, jnp.int32)
        for block in range(2 * REACH + 1):
            lanes = slice(CAP * block, CAP * (block + 1))
            slot_ids[0:1, lanes] = edge_ids[block]
            slot_ids[8:9, lanes] = flip_ids[block]
        own, flip = slot_ids[0:1, :], slot_ids[8:9, :]
        odd = lane_row % 2 == 1
        paired = jnp.where(odd, pltpu.roll(own, 1, 1), pltpu.roll(own, 127, 1))
        inner = (lane_row >= CAP * REACH) & (lane_row < CAP * (REACH + 1))
        given = jnp.where(inner, paired, own)
        edge_row = lax.broadcasted_iota(jnp.int32, (128, 128), 0)
        hot = jnp.where(edge_row == own, 1.0, 0.0).astype(F32)
        recv_hot[:, 0:128] = hot.astype(BF16)
        recv_hot[:, 128:256] = hot.astype(BF16)
        gave = jnp.where(edge_row == given, 1.0, 0.0).astype(F32)
        turned = jnp.where(flip == 1, gave, 0.0)
        straight = (gave - turned).T.astype(BF16)
        turned = turned.T.astype(BF16)
        for part in range(2):
            send_hot[:, 256 * part : 256 * part + 128] = straight
            send_hot[:, 256 * part + 128 : 256 * part + 256] = turned
        counts = jnp.sum(hot.T, axis=0, keepdims=True)
        spread = []
        for edge in range(4):
            one = jnp.where(lane_row // ELEMS == edge, counts, 0.0)
            one = one + pltpu.roll(one, 64, 1)
            spread.append(one + pltpu.roll(one, 32, 1))
        inv_weight[...] = jnp.ones((KROWS, 128), F32)
        for edge, rows in enumerate(edge_rows):
            inv_weight[rows, :] = inv_weight[rows, :] + spread[edge]
        inv_weight[...] = 1.0 / inv_weight[...]
        trace_b[...] = jnp.zeros((40, 256), F32)
        edge_out[...] = jnp.zeros((STEPS, 3, 128, 128), F32)
        edge_in[:, :, 120:128, :] = jnp.zeros((STEPS, 3, 8, 128), F32)

    def physical(step):
        def column(at):
            return jnp.concatenate(
                [
                    recv_out[step, pl.ds(at + mode, PLANE, stride=WIRE), :]
                    for mode in range(LOCAL)
                ],
                axis=0,
            )

        for chunk in range(1 if step == 0 else 3):
            all_out(step, chunk).wait_recv()
        columns = []
        for comp in range(3):
            columns += [column(STATE_AT[step][comp]), column(STATE_AT[step][comp] + LOCAL)]
        of_state = dot(span_in[...], three(jnp.concatenate(columns, axis=1)))

        def flow(base, index):
            row = MODES * (STEPS * index + step)
            return base[row : row + MODES, :]

        def product(comp, base, side, along_x, along_y):
            def now(i, slope=False):
                lanes = 128 * (2 * i + side)
                rows = slice(MODES, 2 * MODES) if slope else slice(0, MODES)
                return of_state[rows, lanes : lanes + 128]

            term = (
                flow(base, 0) * along_x + flow(base, 1) * along_y + flow(base, 2) * now(comp, True)
            )
            return term - (
                now(0) * flow(base, 3 + comp)
                + now(1) * flow(base, 6 + comp)
                + now(2) * flow(base, 9 + comp)
            )

        for comp in range(3):
            if step == 0 or comp == 2:
                all_out(step, comp + 1).wait_recv()
            at = GRAD_AT[step][comp]
            rhs = three(jnp.concatenate([column(at), column(at + LOCAL)], axis=1))
            of_grads = dot(span_in[0:MODES, :], rhs)
            first = product(comp, base_head, 0, of_grads[:, 0:128], of_grads[:, 128:256])
            rest_now = of_state[0:MODES, 128 * (2 * comp + 1) : 128 * (2 * comp + 2)]
            rest = product(comp, base_tail, 1, turn(rest_now, -REST), turn(rest_now, -2 * REST))
            back = dot(fwd_in[...], three(jnp.concatenate([first, rest], axis=1)))
            for at in range(2):
                for mode in range(LOCAL):
                    send_back[step, comp, pl.ds(at * LOCAL + mode, PLANE, stride=BACK), :] = back[
                        PLANE * mode : PLANE * (mode + 1), 128 * at : 128 * at + 128
                    ]
            each_peer(lambda distance, comp=comp: back_copy(step, comp, distance).start())
            mine = pl.ds(pl.multiple_of(me * BACK, 8), BACK)
            recv_back[step, comp, mine, :] = send_back[step, comp, mine, :]

    first_col, last_col = pl.ds(0, NODES, stride=NODES), pl.ds(8, NODES, stride=NODES)
    edge_rows = (first_col, slice(72, 81), last_col, slice(0, 9))

    def update(step, comp):
        all_back(step, comp).wait_recv()

        def came(at):
            return recv_back[step, comp, pl.ds(at, PLANE, stride=BACK), :]

        firsts, lasts = [], []
        for mode in range(LOCAL):
            moved = came(mode)
            last = jnp.where(places[0], came(LOCAL + mode), 0.0)
            firsts.append(jnp.where(after, moved, 0.0))
            lasts.append(jnp.where(after, last, moved))
        for k, rate in enumerate(swap_blocks(firsts) + swap_blocks(lasts)[:2]):
            rows = pl.ds(k, PLANE, stride=5)
            state[comp, rows, :] = state[comp, rows, :] + STEP_SIZE * rate

    def give_edges(step, comp):
        traces = swap_blocks([state[comp, rows, :] for rows in edge_rows])
        for mode in range(LOCAL):
            trace_a[mode * 16 : mode * 16 + NODES, :] = traces[mode]
        for i in range(NODES):
            rows = trace_a[pl.ds(i, LOCAL, stride=16), :]
            trace_b[LOCAL * i : LOCAL * (i + 1), 0:128] = rows
            trace_b[LOCAL * (8 - i) : LOCAL * (9 - i), 128:256] = rows
        hi, lo = halves(trace_b[...])
        given = lax.dot_general(
            send_hot[...],
            jnp.concatenate([hi, lo], axis=1),
            (((1,), (1,)), ((), ())),
            preferred_element_type=F32,
        )
        edge_out[step, comp, :, 0:40] = given
        for block in others:
            edge_copy(step, comp, block).start()
        inner = slice(CAP * REACH, CAP * (REACH + 1))
        edge_in[step, comp, inner, :] = edge_out[step, comp, inner, :]

    def take_edges(step, comp):
        all_edges(step, comp).wait_recv()
        hi, lo = halves(edge_in[step, comp])
        sums[...] = dot(recv_hot[...], jnp.concatenate([hi, lo], axis=0)).T
        parts = swap_blocks([sums[pl.ds(mode, NODES, stride=LOCAL), :] for mode in range(LOCAL)])
        for rows, part in zip(edge_rows, parts):
            state[comp, rows, :] = state[comp, rows, :] + part
        state[comp, 0:ROWS, :] = state[comp, 0:ROWS, :] * inv_weight[0:ROWS, :]

    loads["deriv"].wait()
    halved = [split_state(comp) for comp in range(3)]
    for comp in range(3):
        derive(0, comp, halved[comp])
    gather_base()
    pl.semaphore_wait(barrier, PLANE - 1 + len(others))
    for chunk in range(4):
        send_chunk(0, chunk)
    for chunk in range(4):
        keep_chunk(0, chunk)
    for comp in range(3):
        diffuse(comp, halved[comp])
    arrange_base()
    prepare_edges()
    loads["span"].wait()
    loads["forward"].wait()
    physical(0)
    for comp in range(3):
        update(0, comp)
        give_edges(0, comp)
    halved = []
    for comp in range(3):
        take_edges(0, comp)
        halved.append(split_state(comp))
        derive(1, comp, halved[comp])
        for chunk in (comp,) if comp < 2 else (2, 3):
            send_chunk(1, chunk)
    for chunk in range(4):
        keep_chunk(1, chunk)
    for comp in range(3):
        diffuse(comp, halved[comp])
    physical(1)
    for comp in range(3):
        update(1, comp)
        give_edges(1, comp)
    for step in range(STEPS):
        for chunk in range(4):
            all_out(step, chunk).wait_send()
        for comp in range(3):
            all_back(step, comp).wait_send()
            all_edges(step, comp).wait_send()
    stores = []
    for comp in range(3):
        take_edges(1, comp)
        store = pltpu.make_async_copy(
            state.at[comp, pl.ds(0, NPTS)], out_ref.at[comp], store_sem.at[comp]
        )
        store.start()
        stores.append(store)
    for store in stores:
        store.wait()


def shards(n_dom, adjoint, metric, base_flow, edge_list, flips):
    state_in = jnp.transpose(adjoint, (0, 2, 3, 1, 4)).reshape(3, NPTS, LOCAL, ELEMS)
    base_in = jnp.transpose(base_flow, (1, 0, 2))
    deriv = derivative_tables()
    span, fwd = span_tables()
    dma = pltpu.SemaphoreType.DMA
    result = pl.pallas_call(
        functools.partial(kernel, n_dom),
        out_shape=jax.ShapeDtypeStruct((3, NPTS, 128), F32),
        in_specs=[pl.BlockSpec(memory_space=pltpu.HBM)] * 8,
        out_specs=pl.BlockSpec(memory_space=pltpu.HBM),
        scratch_shapes=[
            pltpu.VMEM((3, KROWS, 128), F32),
            pltpu.VMEM((6, KROWS, 128), F32),
            pltpu.VMEM((12, STEPS, 128 * NPTS), F32),
            pltpu.VMEM((FLOWS * (NPTS + 2), 128), F32),
            pltpu.VMEM((FLOWS * MODES, 128), F32),
            pltpu.VMEM((FLOWS * MODES, 128), F32),
            pltpu.VMEM((STEPS, PLANE * WIRE, 128), F32),
            pltpu.VMEM((STEPS, PLANE * WIRE, 128), F32),
            pltpu.VMEM((STEPS, 3, PLANE * BACK, 128), F32),
            pltpu.VMEM((STEPS, 3, PLANE * BACK, 128), F32),
            pltpu.VMEM((STEPS, 3, 128, 128), F32),
            pltpu.VMEM((STEPS, 3, 128, 128), F32),
            pltpu.VMEM((LOCAL * 16, 128), F32),
            pltpu.VMEM((40, 256), F32),
            pltpu.VMEM((128, 128), F32),
            pltpu.VMEM((128, 512), BF16),
            pltpu.VMEM((128, 256), BF16),
            pltpu.VMEM((KROWS, 128), F32),
            pltpu.VMEM((8, 128), F32),
            pltpu.VMEM((16, 128), jnp.int32),
            pltpu.VMEM((3, NPTS, LOCAL, ELEMS), F32),
            pltpu.VMEM((4, ELEMS), F32),
            pltpu.VMEM(deriv.shape, BF16),
            pltpu.VMEM((2 * REACH + 1, 1, CAP), jnp.int32),
            pltpu.VMEM((2 * REACH + 1, 1, CAP), jnp.int32),
            pltpu.VMEM(span.shape, BF16),
            pltpu.VMEM(fwd.shape, BF16),
            dma((8,)),
            dma((3,)),
            dma((STEPS, 4)),
            dma((STEPS, 4)),
            dma((STEPS, 3)),
            dma((STEPS, 3)),
            dma((STEPS, 3)),
            dma((STEPS, 3)),
        ],
        compiler_params=pltpu.CompilerParams(
            collective_id=0, has_side_effects=True, vmem_limit_bytes=58 * 1024 * 1024
        ),
    )(
        state_in,
        metric,
        base_in,
        jnp.transpose(edge_list, (1, 0, 2)),
        jnp.transpose(flips, (1, 0, 2)),
        jnp.asarray(deriv),
        jnp.asarray(span),
        jnp.asarray(fwd),
    )
    return jnp.transpose(result.reshape(3, NODES, NODES, LOCAL, ELEMS), (0, 3, 1, 2, 4))


def solution(mesh):
    placed = (
        P(None, "plane", None, None, "dom"),
        P(None, "dom"),
        P(None, None, ("dom", "plane")),
        P("dom", None, None),
        P("dom", None, None),
    )
    return jax.shard_map(
        functools.partial(shards, mesh.shape["dom"]),
        mesh=mesh,
        in_specs=placed,
        out_specs=P(None, "plane", None, None, "dom"),
        check_vma=False,
    )
```
